512 devices in a mesh: row: 16 (over x, z_hi, core), col: 32 (over y, z_lo).
Axes of the slice: x: 4, y: 4, z: 16 (z_hi: 2, z_lo: 8; z = z_hi * 8 + z_lo), core: 2. Of those that a mesh axis runs over, the one named last changes fastest.
Arguments:
- pair: bfloat16 [768, 768, 128], P('row', 'col'), may hold values from -6 to 6
- token_mask: int32 [768], P('col'), may hold values from 0 to 1, as said below
- w_query: bfloat16 [128, 128], replicated, may hold values from -0.5 to 0.5
- w_key: bfloat16 [128, 128], replicated, may hold values from -0.5 to 0.5
- w_value: bfloat16 [128, 128], replicated, may hold values from -0.5 to 0.5
- w_gate: bfloat16 [128, 128], replicated, may hold values from -0.5 to 0.5
- w_bias: bfloat16 [128, 4], replicated
- w_out: bfloat16 [128, 128], replicated, may hold values from -0.5 to 0.5
- w_hidden_a: bfloat16 [128, 512], replicated, may hold values from -0.5 to 0.5
- w_hidden_b: bfloat16 [128, 512], replicated, may hold values from -0.5 to 0.5
- w_hidden_out: bfloat16 [512, 128], replicated, may hold values from -0.25 to 0.25
Outputs:
- updated_rows: bfloat16 [320, 768, 128], P('row', 'col')
The draws below stay inside these ranges and needn't reach their ends.
Inputs may be any that keep to these rules, and one draw needn't show every extreme that they name: `token_mask`: the 768 residues fall into aligned blocks of 64; in each block the first 16 to 64 residues are 1 and the rest 0.
All inputs are finite; a program needn't handle non-finite values.
Results may differ from the reference program's by a relative error of at most 0.011.
The reference program's roundings to bfloat16 on the way count: a program that leaves them out, or rounds other values in their place, can miss the bound.
Values may be sent and summed in bfloat16 or wider, within the bound.
A program may use at most 64 MiB of HBM per device.

```python
import jax
import jax.numpy as jnp
from jax import lax

C = 128
HEADS = 4
HEAD_DIM = 32
HT = 512
QR = 20
N = 768
RB = 48
QROWS = 320
N_ROW = 16


def draw_w_bias(key, part):
    own_key = jax.random.fold_in(key, 11)
    base = jax.random.normal(own_key, (C, HEADS), jnp.float32)
    return (base * 0.25).astype(jnp.bfloat16)


def draw_token_mask(key, part):
    own_key = jax.random.fold_in(key, 23)
    blocks = N // 64
    lengths = jax.random.randint(own_key, (blocks, 1), 16, 65)
    position = jnp.arange(64, dtype=jnp.int32)[None, :]
    return (position < lengths).astype(jnp.int32).reshape(N)


def steps_of(key, shape, split, low, high):
    loudness = 1.0
    for dim, shards_of in split:
        heights = jax.random.uniform(jax.random.fold_in(jax.random.fold_in(key, 6), dim), (shards_of,), jnp.float32, low / len(split), high / len(split))
        loudness = loudness * jnp.repeat(jnp.exp(heights), shape[dim] // shards_of).reshape((-1,) + (1,) * (len(shape) - 1 - dim))
    return loudness


def normal_values(rng, extent, scale, most, split=(), kind=jnp.bfloat16):
    array = jax.random.normal(rng, extent, jnp.float32) * scale
    if len(split) > 0:
        array = steps_of(rng, extent, split, -0.22, 0.18) * array
    return jnp.clip(array, min=-most, max=most).astype(kind)


def setup_inputs(seed: int = 0) -> dict:
    keys = jax.random.split(jax.random.key(seed), 12)
    pair = normal_values(keys[0], (N, N, C), 1.0, 6.0, ((0, 16), (1, 32)))
    token_mask = draw_token_mask(jax.random.fold_in(keys[11], 71), 0)
    w_query = normal_values(keys[2], (C, HEADS * HEAD_DIM), C ** -0.5, 0.5)
    w_key = normal_values(keys[3], (C, HEADS * HEAD_DIM), C ** -0.5, 0.5)
    w_value = normal_values(keys[4], (C, HEADS * HEAD_DIM), C ** -0.5, 0.5)
    w_gate = normal_values(keys[5], (C, HEADS * HEAD_DIM), C ** -0.5, 0.5)
    w_bias = draw_w_bias(jax.random.fold_in(keys[11], 71), 0)
    w_out = normal_values(keys[7], (HEADS * HEAD_DIM, C), (HEADS * HEAD_DIM) ** -0.5, 0.5)
    w_hidden_a = normal_values(keys[8], (C, HT), C ** -0.5, 0.5)
    w_hidden_b = normal_values(keys[9], (C, HT), C ** -0.5, 0.5)
    w_hidden_out = normal_values(keys[10], (HT, C), HT ** -0.5, 0.25)
    return dict(pair=pair, token_mask=token_mask, w_query=w_query, w_key=w_key, w_value=w_value, w_gate=w_gate, w_bias=w_bias, w_out=w_out, w_hidden_a=w_hidden_a, w_hidden_b=w_hidden_b, w_hidden_out=w_hidden_out)


def normalize(values_in):
    average = lax.optimization_barrier(jnp.mean(values_in, axis=-1, keepdims=True))
    centred = values_in - average
    variance = lax.optimization_barrier(jnp.mean(centred * centred, axis=-1, keepdims=True))
    return centred * lax.rsqrt(variance + 1e-05)

def reference(pair, token_mask, w_query, w_key, w_value, w_gate, w_bias, w_out, w_hidden_a, w_hidden_b, w_hidden_out):
    normed = lax.map(lambda pair_row: normalize(pair_row.astype(jnp.float32)).astype(jnp.bfloat16), pair)
    bias_flat = jnp.dot(normed.reshape(-1, C), w_bias, preferred_element_type=jnp.float32).astype(jnp.bfloat16)
    bias = bias_flat.reshape(N, N, HEADS).transpose(2, 0, 1)
    window_raw = pair.reshape(N_ROW, RB, N, C)[:, :QR].reshape(QROWS, N, C)
    window_normed = normed.reshape(N_ROW, RB, N, C)[:, :QR].reshape(QROWS, N, C)
    alive = token_mask > 0
    score_scale = 1.0 / math_sqrt(HEAD_DIM)

    def one_row(inputs):
        raw_row, normed_row = inputs
        queries = (jnp.dot(normed_row, w_query, preferred_element_type=jnp.float32) * score_scale).astype(jnp.bfloat16)
        keys_row = jnp.dot(normed_row, w_key, preferred_element_type=jnp.float32).astype(jnp.bfloat16)
        values_row = jnp.dot(normed_row, w_value, preferred_element_type=jnp.float32).astype(jnp.bfloat16)
        gate_logits = jnp.dot(normed_row, w_gate, preferred_element_type=jnp.float32)
        queries = queries.reshape(N, HEADS, HEAD_DIM).astype(jnp.float32)
        keys_row = keys_row.reshape(N, HEADS, HEAD_DIM).astype(jnp.float32)
        values_row = values_row.reshape(N, HEADS, HEAD_DIM).astype(jnp.float32)
        scores = jnp.einsum('jhd,khd->hjk', queries, keys_row) + bias.astype(jnp.float32)
        masked = jnp.where(alive, scores, jnp.float32(-1e+30))
        top = lax.optimization_barrier(jnp.max(masked, axis=-1, keepdims=True))
        weights = jnp.where(alive, jnp.exp(scores - top), jnp.float32(0.0))
        total = lax.optimization_barrier(jnp.sum(weights, axis=-1))
        rounded = lax.optimization_barrier(weights.astype(jnp.bfloat16)).astype(jnp.float32)
        attended = jnp.einsum('hjk,khd->jhd', rounded, values_row) / total.T[:, :, None]
        gated = (jax.nn.sigmoid(gate_logits) * attended.reshape(N, HEADS * HEAD_DIM)).astype(jnp.bfloat16)
        first = raw_row.astype(jnp.float32) + jnp.dot(gated, w_out, preferred_element_type=jnp.float32)
        normed_two = normalize(first).astype(jnp.bfloat16)
        hidden = (jax.nn.silu(jnp.dot(normed_two, w_hidden_a, preferred_element_type=jnp.float32)) * jnp.dot(normed_two, w_hidden_b, preferred_element_type=jnp.float32)).astype(jnp.bfloat16)
        return (first + jnp.dot(hidden, w_hidden_out, preferred_element_type=jnp.float32)).astype(jnp.bfloat16)
    return lax.map(one_row, (window_raw, window_normed))

def math_sqrt(number):
    return float(number) ** 0.5
```

```python
import functools
import math

import jax
import jax.numpy as jnp
from jax import lax
from jax.experimental import pallas as pl
from jax.experimental.pallas import tpu as pltpu
from jax.sharding import PartitionSpec as P

HEADS = 4
HEAD_DIM = 32
QR = 20
NZ = 8
NY = 4
DEAD = -1e30
MESH = pl.DeviceIdType.MESH
F32 = jnp.float32
BF16 = jnp.bfloat16


def normalize(values_in):
    average = jnp.mean(values_in, axis=-1, keepdims=True)
    centred = values_in - average
    variance = jnp.mean(centred * centred, axis=-1, keepdims=True)
    return centred * lax.rsqrt(variance + 1e-05)


def dot(a, b):
    return jnp.dot(a, b, preferred_element_type=F32)


def dot_t(a, b):
    return lax.dot_general(a, b, (((1,), (1,)), ((), ())), preferred_element_type=F32)


def sigmoid(v):
    return 1.0 / (1.0 + jnp.exp(-v))


def kernel(
    columns,
    pair_ref,
    mask_ref,
    wq_ref,
    wk_ref,
    wv_ref,
    wg_ref,
    wb_ref,
    wo_ref,
    wha_ref,
    whb_ref,
    who_ref,
    out_ref,
    gath,
    part,
    biasg,
    bias_t,
    qk_ref,
    m_ref,
    l_ref,
    acc_ref,
    b_own,
    send_g,
    recv_g,
    send_b1,
    recv_b1,
    send_b2,
    recv_b2,
):
    rows_block = pair_ref.shape[0]
    channels = pair_ref.shape[2]
    tokens = QR * columns
    hq = HEADS * columns
    row = lax.axis_index("row")
    col = lax.axis_index("col")
    y = col // NZ
    z = col % NZ
    yp = (y + 1) % NY
    ym = (y + NY - 1) % NY
    y2 = (y + 2) % NY
    core = row % 2
    grp = row // 2
    my_q = (col % 2) * 2 + core

    def b1_dest(g):
        return 2 * g + col % 2, 2 * row + (col // 2) % 2

    def b1_source(n):
        return col // 2, 4 * n + (col % 2) * 2 + core

    def quad(d):
        q = (my_q + d) % 4
        return 2 * grp + q % 2, 2 * (col // 2) + q // 2, q

    barrier = pltpu.get_barrier_semaphore()

    def greet(r, c):
        pl.semaphore_signal(barrier, inc=1, device_id=(r, c), device_id_type=MESH)

    greet(row, yp * NZ + z)
    greet(row, ym * NZ + z)

    @pl.when(z < NZ - 1)
    def _():
        greet(row, col + 1)

    @pl.when(z > 0)
    def _():
        greet(row, col - 1)

    for d in range(1, 4):
        qr_, qc_, _q = quad(d)
        greet(qr_, qc_)
    for n in range(8):
        sr_, sc_ = b1_source(n)

        @pl.when(jnp.logical_or(sr_ != row, sc_ != col))
        def _():
            greet(sr_, sc_)

    win = normalize(pair_ref[:QR].astype(F32)).astype(BF16)
    gath[col] = win

    is_own = jnp.logical_and(row == 2 * (row // 2) + col % 2, col == 2 * row + (col // 2) % 2)
    greeted = 2 + 3 + 8 + (z < NZ - 1).astype(jnp.int32) + (z > 0).astype(jnp.int32)
    greeted = greeted - is_own.astype(jnp.int32)
    pl.semaphore_wait(barrier, greeted)

    def hop(direction, s):
        r, c = row, {0: col + 1, 1: col - 1, 2: yp * NZ + z, 3: ym * NZ + z}[direction]
        return pltpu.make_async_remote_copy(
            src_ref=gath.at[s],
            dst_ref=gath.at[s],
            send_sem=send_g.at[direction, s],
            recv_sem=recv_g.at[s],
            device_id=(r, c),
            device_id_type=MESH,
        )

    def arrived(s):
        pltpu.make_async_copy(gath.at[s], gath.at[s], recv_g.at[s]).wait()

    def move(t):
        zr = z - t
        zl = z + t
        sr = y * NZ + zr
        sl = y * NZ + zl

        @pl.when(zr >= 0)
        def _():
            if t > 0:
                arrived(sr)

            @pl.when(z < NZ - 1)
            def _():
                hop(0, sr).start()

            if t == 0:

                @pl.when(z > 0)
                def _():
                    hop(1, sr).start()

            hop(2, sr).start()
            hop(3, sr).start()

        if t > 0:

            @pl.when(zl < NZ)
            def _():
                arrived(sl)

                @pl.when(z > 0)
                def _():
                    hop(1, sl).start()

                hop(2, sl).start()
                hop(3, sl).start()

    def pass_on(t):
        def one(zz):
            @pl.when(zz % 2 == 0)
            def _():
                arrived(ym * NZ + zz)
                hop(2, ym * NZ + zz).start()

            @pl.when(zz % 2 == 1)
            def _():
                arrived(yp * NZ + zz)
                hop(3, yp * NZ + zz).start()

        @pl.when(z - t >= 0)
        def _():
            one(z - t)

        if t > 0:

            @pl.when(z + t < NZ)
            def _():
                one(z + t)

    move(0)

    lane = lax.broadcasted_iota(jnp.int32, (columns, channels), 1)
    head_of = sum((lane >= columns * (h + 1)).astype(jnp.int32) for h in range(HEADS))
    lane_mod = lane - head_of * columns
    lane_w = lax.broadcasted_iota(jnp.int32, (channels, channels), 1)
    wb = wb_ref[...].astype(F32)
    wide = jnp.zeros((channels, channels), F32)
    for h in range(HEADS):
        inside = jnp.logical_and(lane_w >= h * columns, lane_w < (h + 1) * columns)
        wide = jnp.where(inside, wb[:, h : h + 1], wide)
    wide = wide.astype(BF16)
    mask_row = mask_ref[...].astype(F32)
    eye = lax.broadcasted_iota(jnp.int32, (columns, columns), 0) == lax.broadcasted_iota(
        jnp.int32, (columns, columns), 1
    )
    alive = jnp.sum(jnp.where(eye, mask_row, 0.0), axis=1, keepdims=True)
    for half in range(2):
        normed = normalize(pair_ref[half * columns : (half + 1) * columns].astype(F32))
        full = dot(normed.reshape(columns * columns, channels).astype(BF16), wide)
        full = full.reshape(columns, columns, channels)
        picked = jnp.zeros((columns, channels), F32)
        for j in range(columns):
            picked = jnp.where(lane_mod == j, full[j], picked)
        picked = jnp.where(alive > 0.0, picked, DEAD)
        b_own[half] = picked.astype(BF16)

    my_n = col // 4

    def b1_copy(g):
        r, c = b1_dest(g)
        return pltpu.make_async_remote_copy(
            src_ref=b_own,
            dst_ref=part.at[my_n],
            send_sem=send_b1.at[g],
            recv_sem=recv_b1.at[my_n],
            device_id=(r, c),
            device_id_type=MESH,
        )

    def b1_self():
        return pltpu.make_async_copy(b_own, part.at[my_n], recv_b1.at[my_n])

    for g in range(8):
        r_, c_ = b1_dest(g)
        here = jnp.logical_and(r_ == row, c_ == col)

        @pl.when(here)
        def _():
            b1_self().start()

        @pl.when(jnp.logical_not(here))
        def _():
            b1_copy(g).start()

    move(1)
    pass_on(0)

    flat = win.astype(F32).reshape(tokens, channels).astype(BF16)
    q = (dot(flat, wq_ref[...]) * (1.0 / math.sqrt(HEAD_DIM))).astype(BF16)
    lane_t = lax.broadcasted_iota(jnp.int32, (tokens, channels), 1)
    for h in range(HEADS):
        inside = jnp.logical_and(lane_t >= h * HEAD_DIM, lane_t < (h + 1) * HEAD_DIM)
        mine = jnp.where(inside, q.astype(F32), 0.0).astype(BF16)
        qk_h = dot_t(mine, wk_ref[...])
        qk_ref[:, h * columns : (h + 1) * columns, :] = qk_h.reshape(QR, columns, channels)

    for n in range(8):
        pltpu.make_async_copy(part.at[n], part.at[n], recv_b1.at[n]).wait()

    def b2_copy(d):
        r, c, q_ = quad(d)
        return pltpu.make_async_remote_copy(
            src_ref=part.at[:, q_ // 2],
            dst_ref=biasg.at[my_q],
            send_sem=send_b2.at[d],
            recv_sem=recv_b2.at[my_q],
            device_id=(r, c),
            device_id_type=MESH,
        )

    for d in range(1, 4):
        b2_copy(d).start()
    biasg[my_q] = part[:, col % 2]

    for t in range(2, NZ):
        move(t)
        pass_on(t - 1)

    for d in range(1, 4):
        q_ = (my_q + d) % 4
        pltpu.make_async_copy(biasg.at[q_], biasg.at[q_], recv_b2.at[q_]).wait()
    for yy in range(NY):
        block = biasg[:, 2 * yy : 2 * yy + 2].astype(F32)
        block = jnp.swapaxes(block, 0, 1).reshape(NZ * columns, channels)
        bias_t[yy] = jnp.swapaxes(block, 0, 1)[:hq]

    def attend(yy, first):
        def body(step, carry):
            for u in range(4):
                i = step * 4 + u
                block = gath[pl.ds(yy * NZ, NZ), i].astype(F32).reshape(NZ * columns, channels).astype(BF16)
                s = dot_t(qk_ref[i].astype(BF16), block) + bias_t[yy]
                top = jnp.max(s, axis=1, keepdims=True)
                if not first:
                    old = m_ref[i][:, :1]
                    top = jnp.maximum(old, top)
                p = jnp.exp(s - top)
                total = jnp.sum(p, axis=1, keepdims=True)
                weighted = dot(p.astype(BF16), block)
                if not first:
                    factor = jnp.exp(old - top)
                    total = total + l_ref[i][:, :1] * factor
                    weighted = weighted + acc_ref[i] * factor
                m_ref[i] = jnp.broadcast_to(top, (hq, channels))
                l_ref[i] = jnp.broadcast_to(total, (hq, channels))
                acc_ref[i] = weighted
            return carry

        lax.fori_loop(0, QR // 4, body, 0)

    attend(y, True)
    pass_on(NZ - 1)
    for zz in range(1, NZ, 2):
        arrived(ym * NZ + zz)
    attend(ym, False)
    for zz in range(0, NZ, 2):
        arrived(yp * NZ + zz)
    attend(yp, False)
    for zz in range(NZ):
        arrived(y2 * NZ + zz)
    attend(y2, False)

    lane_t = lax.broadcasted_iota(jnp.int32, (tokens, channels), 1)
    mean_n = acc_ref[...] / l_ref[...]
    attended = jnp.zeros((tokens, channels), F32)
    for h in range(HEADS):
        mine = mean_n[:, h * columns : (h + 1) * columns].reshape(tokens, channels).astype(BF16)
        inside = jnp.logical_and(lane_t >= h * HEAD_DIM, lane_t < (h + 1) * HEAD_DIM)
        attended = jnp.where(inside, dot(mine, wv_ref[...]), attended)
    flat = gath[col].astype(F32).reshape(tokens, channels).astype(BF16)
    gated = (sigmoid(dot(flat, wg_ref[...])) * attended).astype(BF16)
    first = pair_ref[:QR].astype(F32).reshape(tokens, channels) + dot(gated, wo_ref[...])
    normed_two = normalize(first).astype(BF16)
    a = dot(normed_two, wha_ref[...])
    b = dot(normed_two, whb_ref[...])
    hidden = (a * sigmoid(a) * b).astype(BF16)
    updated = first + dot(hidden, who_ref[...])
    out_ref[...] = updated.reshape(QR, columns, channels).astype(out_ref.dtype)

    def sent(direction, s):
        pltpu.make_async_copy(gath.at[s], gath.at[s], send_g.at[direction, s]).wait()

    for zz in range(NZ):
        s = y * NZ + zz

        @pl.when(jnp.logical_and(zz <= z, z < NZ - 1))
        def _():
            sent(0, s)

        @pl.when(jnp.logical_and(zz >= z, z > 0))
        def _():
            sent(1, s)

        sent(2, s)
        sent(3, s)
        if zz % 2 == 0:
            sent(2, ym * NZ + zz)
        else:
            sent(3, yp * NZ + zz)
    for g in range(8):
        r_, c_ = b1_dest(g)

        @pl.when(jnp.logical_or(r_ != row, c_ != col))
        def _():
            b1_copy(g).wait_send()

    for d in range(1, 4):
        b2_copy(d).wait_send()


def local(pair, token_mask, *weights):
    rows_block, columns, channels = pair.shape
    hq = HEADS * columns
    cols = NY * NZ
    dma = pltpu.SemaphoreType.DMA
    return pl.pallas_call(
        functools.partial(kernel, columns),
        out_shape=jax.ShapeDtypeStruct((QR, columns, channels), BF16),
        in_specs=[pl.BlockSpec(memory_space=pltpu.VMEM)] * 11,
        out_specs=pl.BlockSpec(memory_space=pltpu.VMEM),
        scratch_shapes=[
            pltpu.VMEM((cols, QR, columns, channels), BF16),
            pltpu.VMEM((8, 2, columns, channels), BF16),
            pltpu.VMEM((4, 8, columns, channels), BF16),
            pltpu.VMEM((NY, hq, NZ * columns), F32),
            pltpu.VMEM((QR, hq, channels), F32),
            pltpu.VMEM((QR, hq, channels), F32),
            pltpu.VMEM((QR, hq, channels), F32),
            pltpu.VMEM((QR, hq, channels), F32),
            pltpu.VMEM((2, columns, channels), BF16),
            dma((4, cols)),
            dma((cols,)),
            dma((8,)),
            dma((8,)),
            dma((4,)),
            dma((4,)),
        ],
        compiler_params=pltpu.CompilerParams(
            collective_id=0, has_side_effects=True, vmem_limit_bytes=48 * 1024 * 1024
        ),
    )(pair, token_mask.reshape(1, columns), *weights)


def solution(mesh):
    return jax.shard_map(
        local,
        mesh=mesh,
        in_specs=(P("row", "col", None), P("col"), P(), P(), P(), P(), P(), P(), P(), P(), P()),
        out_specs=P("row", "col", None),
        check_vma=False,
    )
```

```python
import functools
import math

import jax
import jax.numpy as jnp
from jax import lax
from jax.experimental import pallas as pl
from jax.experimental.pallas import tpu as pltpu
from jax.sharding import PartitionSpec as P

HEADS = 4
HEAD_DIM = 32
QR = 20
NZ = 8
NY = 4
CHUNKS = 1
UNROLL = 4
DEAD = -1e30
MESH = pl.DeviceIdType.MESH
F32 = jnp.float32
BF16 = jnp.bfloat16


def normalize(values_in):
    average = jnp.mean(values_in, axis=-1, keepdims=True)
    centred = values_in - average
    variance = jnp.mean(centred * centred, axis=-1, keepdims=True)
    return centred * lax.rsqrt(variance + 1e-05)


def dot(a, b):
    return jnp.dot(a, b, preferred_element_type=F32)


def dot_t(a, b):
    return lax.dot_general(a, b, (((1,), (1,)), ((), ())), preferred_element_type=F32)


def sigmoid(v):
    return 1.0 / (1.0 + jnp.exp(-v))


def kernel(
    columns,
    *refs,
):
    inputs, out_ref, held = refs[:11], refs[11], refs[12:23]
    pair_ref, mask_ref, wq_ref, wk_ref, wv_ref, wg_ref, wb_ref, wo_ref, wha_ref, whb_ref, who_ref = held
    body(
        columns,
        inputs,
        held,
        pair_ref,
        mask_ref,
        wq_ref,
        wk_ref,
        wv_ref,
        wg_ref,
        wb_ref,
        wo_ref,
        wha_ref,
        whb_ref,
        who_ref,
        out_ref,
        *refs[23:],
    )


def body(
    columns,
    inputs,
    held,
    pair_ref,
    mask_ref,
    wq_ref,
    wk_ref,
    wv_ref,
    wg_ref,
    wb_ref,
    wo_ref,
    wha_ref,
    whb_ref,
    who_ref,
    out_ref,
    gath,
    part,
    biasg,
    bias_t,
    qk_ref,
    m_ref,
    l_ref,
    acc_ref,
    b_own,
    send_g,
    recv_g,
    send_b1,
    recv_b1,
    send_b2,
    recv_b2,
    load_sem,
):
    rows_block = pair_ref.shape[0]
    channels = pair_ref.shape[2]
    tokens = QR * columns
    hq = HEADS * columns
    row = lax.axis_index("row")
    col = lax.axis_index("col")
    y = col // NZ
    z = col % NZ
    yp = (y + 1) % NY
    ym = (y + NY - 1) % NY
    y2 = (y + 2) % NY
    core = row % 2
    grp = row // 2
    my_q = (col % 2) * 2 + core

    def b1_dest(g):
        return 2 * g + col % 2, 2 * row + (col // 2) % 2

    def b1_source(n):
        return col // 2, 4 * n + (col % 2) * 2 + core

    def quad(d):
        q = (my_q + d) % 4
        return 2 * grp + q % 2, 2 * (col // 2) + q // 2, q

    def load(n):
        if n == 0:
            return pltpu.make_async_copy(inputs[0].at[:QR], pair_ref.at[:QR], load_sem.at[0])
        if n == 11:
            rest = pl.ds(QR, rows_block - QR)
            return pltpu.make_async_copy(inputs[0].at[rest], pair_ref.at[rest], load_sem.at[11])
        return pltpu.make_async_copy(inputs[n], held[n], load_sem.at[n])

    for n in (0, 11, 6, 1, 2, 3, 4, 5, 7, 8, 9, 10):
        load(n).start()

    barrier = pltpu.get_barrier_semaphore()

    def greet(r, c):
        pl.semaphore_signal(barrier, inc=1, device_id=(r, c), device_id_type=MESH)

    greet(row, yp * NZ + z)
    greet(row, ym * NZ + z)

    @pl.when(z < NZ - 1)
    def _():
        greet(row, col + 1)

    @pl.when(z > 0)
    def _():
        greet(row, col - 1)

    for d in range(1, 4):
        qr_, qc_, _q = quad(d)
        greet(qr_, qc_)
    for n in range(8):
        sr_, sc_ = b1_source(n)

        @pl.when(jnp.logical_or(sr_ != row, sc_ != col))
        def _():
            greet(sr_, sc_)

    load(0).wait()
    win = normalize(pair_ref[:QR].astype(F32)).astype(BF16)
    gath[col] = win

    is_own = jnp.logical_and(row == 2 * (row // 2) + col % 2, col == 2 * row + (col // 2) % 2)
    greeted = 2 + 3 + 8 + (z < NZ - 1).astype(jnp.int32) + (z > 0).astype(jnp.int32)
    greeted = greeted - is_own.astype(jnp.int32)
    pl.semaphore_wait(barrier, greeted)

    def hop(direction, s):
        r, c = row, {0: col + 1, 1: col - 1, 2: yp * NZ + z, 3: ym * NZ + z}[direction]
        return pltpu.make_async_remote_copy(
            src_ref=gath.at[s],
            dst_ref=gath.at[s],
            send_sem=send_g.at[direction, s],
            recv_sem=recv_g.at[s],
            device_id=(r, c),
            device_id_type=MESH,
        )

    def arrived(s):
        pltpu.make_async_copy(gath.at[s], gath.at[s], recv_g.at[s]).wait()

    def move(t):
        zr = z - t
        zl = z + t
        sr = y * NZ + zr
        sl = y * NZ + zl

        @pl.when(zr >= 0)
        def _():
            if t > 0:
                arrived(sr)

            @pl.when(z < NZ - 1)
            def _():
                hop(0, sr).start()

            if t == 0:

                @pl.when(z > 0)
                def _():
                    hop(1, sr).start()

            hop(2, sr).start()
            hop(3, sr).start()

        if t > 0:

            @pl.when(zl < NZ)
            def _():
                arrived(sl)

                @pl.when(z > 0)
                def _():
                    hop(1, sl).start()

                hop(2, sl).start()
                hop(3, sl).start()

    def pass_on(t):
        def one(zz):
            @pl.when(zz % 2 == 0)
            def _():
                arrived(ym * NZ + zz)
                hop(2, ym * NZ + zz).start()

            @pl.when(zz % 2 == 1)
            def _():
                arrived(yp * NZ + zz)
                hop(3, yp * NZ + zz).start()

        @pl.when(z - t >= 0)
        def _():
            one(z - t)

        if t > 0:

            @pl.when(z + t < NZ)
            def _():
                one(z + t)

    move(0)

    lane = lax.broadcasted_iota(jnp.int32, (columns, channels), 1)
    head_of = sum((lane >= columns * (h + 1)).astype(jnp.int32) for h in range(HEADS))
    lane_mod = lane - head_of * columns
    for n in (11, 6, 1):
        load(n).wait()
    wb = wb_ref[...].astype(F32)
    wide = [jnp.broadcast_to(wb[h : h + 1], (columns, channels)) for h in range(HEADS)]
    wide = jnp.concatenate(wide + [jnp.zeros((channels - hq, channels), F32)], axis=0).astype(BF16)
    mask_row = mask_ref[...].astype(F32)
    eye = lax.broadcasted_iota(jnp.int32, (columns, columns), 0) == lax.broadcasted_iota(
        jnp.int32, (columns, columns), 1
    )
    alive = jnp.sum(jnp.where(eye, mask_row, 0.0), axis=1, keepdims=True)
    for half in range(2):
        normed = normalize(pair_ref[half * columns : (half + 1) * columns].astype(F32))
        full = dot_t(normed.reshape(columns * columns, channels).astype(BF16), wide)
        full = full.reshape(columns, columns, channels)
        picked = jnp.zeros((columns, channels), F32)
        for j in range(columns):
            picked = jnp.where(lane_mod == j, full[j], picked)
        picked = jnp.where(alive > 0.0, picked, DEAD)
        b_own[half] = picked.astype(BF16)

    my_n = col // 4

    def b1_copy(g):
        r, c = b1_dest(g)
        return pltpu.make_async_remote_copy(
            src_ref=b_own,
            dst_ref=part.at[my_n],
            send_sem=send_b1.at[g],
            recv_sem=recv_b1.at[my_n],
            device_id=(r, c),
            device_id_type=MESH,
        )

    def b1_self():
        return pltpu.make_async_copy(b_own, part.at[my_n], recv_b1.at[my_n])

    for g in range(8):
        r_, c_ = b1_dest(g)
        here = jnp.logical_and(r_ == row, c_ == col)

        @pl.when(here)
        def _():
            b1_self().start()

        @pl.when(jnp.logical_not(here))
        def _():
            b1_copy(g).start()

    move(1)
    pass_on(0)

    for n in (2, 3):
        load(n).wait()
    flat = win.astype(F32).reshape(tokens, channels).astype(BF16)
    q = (dot(flat, wq_ref[...]) * (1.0 / math.sqrt(HEAD_DIM))).astype(BF16)
    lane_t = lax.broadcasted_iota(jnp.int32, (tokens, channels), 1)
    for h in range(HEADS):
        inside = jnp.logical_and(lane_t >= h * HEAD_DIM, lane_t < (h + 1) * HEAD_DIM)
        mine = jnp.where(inside, q.astype(F32), 0.0).astype(BF16)
        qk_h = dot_t(mine, wk_ref[...])
        qk_ref[:, h * columns : (h + 1) * columns, :] = qk_h.reshape(QR, columns, channels)

    for n in range(8):
        pltpu.make_async_copy(part.at[n], part.at[n], recv_b1.at[n]).wait()

    def b2_copy(d):
        r, c, q_ = quad(d)
        return pltpu.make_async_remote_copy(
            src_ref=part.at[:, q_ // 2],
            dst_ref=biasg.at[my_q],
            send_sem=send_b2.at[d],
            recv_sem=recv_b2.at[my_q],
            device_id=(r, c),
            device_id_type=MESH,
        )

    for d in range(1, 4):
        b2_copy(d).start()
    biasg[my_q] = part[:, col % 2]

    for t in range(2, NZ):
        move(t)
        pass_on(t - 1)

    for d in range(1, 4):
        q_ = (my_q + d) % 4
        pltpu.make_async_copy(biasg.at[q_], biasg.at[q_], recv_b2.at[q_]).wait()
    wave = NY // CHUNKS
    keys = wave * NZ * columns
    for part_no in range(CHUNKS):
        block = biasg[:, 2 * wave * part_no : 2 * wave * (part_no + 1)].astype(F32)
        block = jnp.swapaxes(block, 0, 1).reshape(keys, channels)
        bias_t[part_no] = jnp.swapaxes(block, 0, 1)[:hq]

    def attend(part_no, first):
        def one(i):
            block = gath[pl.ds(part_no * wave * NZ, wave * NZ), i].astype(F32)
            block = block.reshape(keys, channels).astype(BF16)
            s = dot_t(qk_ref[i].astype(BF16), block) + bias_t[part_no]
            top = jnp.broadcast_to(jnp.max(s, axis=1, keepdims=True), (hq, channels))
            if not first:
                old = m_ref[i]
                top = jnp.maximum(old, top)
            p = jnp.exp(s - jnp.concatenate([top] * (keys // channels), axis=1))
            total = jnp.broadcast_to(jnp.sum(p, axis=1, keepdims=True), (hq, channels))
            weighted = dot(p.astype(BF16), block)
            if not first:
                factor = jnp.exp(old - top)
                total = total + l_ref[i] * factor
                weighted = weighted + acc_ref[i] * factor
            if CHUNKS > 1 and first:
                m_ref[i] = top
            l_ref[i] = total
            acc_ref[i] = weighted

        def several(step, carry):
            for u in range(UNROLL):
                one(step * UNROLL + u)
            return carry

        lax.fori_loop(0, QR // UNROLL, several, 0)

    pass_on(NZ - 1)
    for zz in range(1, NZ, 2):
        arrived(ym * NZ + zz)
    for zz in range(0, NZ, 2):
        arrived(yp * NZ + zz)
    for zz in range(NZ):
        arrived(y2 * NZ + zz)
    attend(0, True)

    for n in (4, 5, 7, 8, 9, 10):
        load(n).wait()
    lane_t = lax.broadcasted_iota(jnp.int32, (tokens, channels), 1)
    mean_n = acc_ref[...] / l_ref[...]
    attended = jnp.zeros((tokens, channels), F32)
    for h in range(HEADS):
        mine = mean_n[:, h * columns : (h + 1) * columns].reshape(tokens, channels).astype(BF16)
        inside = jnp.logical_and(lane_t >= h * HEAD_DIM, lane_t < (h + 1) * HEAD_DIM)
        attended = jnp.where(inside, dot(mine, wv_ref[...]), attended)
    flat = gath[col].astype(F32).reshape(tokens, channels).astype(BF16)
    gated = (sigmoid(dot(flat, wg_ref[...])) * attended).astype(BF16)
    first = pair_ref[:QR].astype(F32).reshape(tokens, channels) + dot(gated, wo_ref[...])
    normed_two = normalize(first).astype(BF16)
    a = dot(normed_two, wha_ref[...])
    b = dot(normed_two, whb_ref[...])
    hidden = (a * sigmoid(a) * b).astype(BF16)
    updated = first + dot(hidden, who_ref[...])
    out_ref[...] = updated.reshape(QR, columns, channels).astype(out_ref.dtype)

    def sent(direction, s):
        pltpu.make_async_copy(gath.at[s], gath.at[s], send_g.at[direction, s]).wait()

    for zz in range(NZ):
        s = y * NZ + zz

        @pl.when(jnp.logical_and(zz <= z, z < NZ - 1))
        def _():
            sent(0, s)

        @pl.when(jnp.logical_and(zz >= z, z > 0))
        def _():
            sent(1, s)

        sent(2, s)
        sent(3, s)
        if zz % 2 == 0:
            sent(2, ym * NZ + zz)
        else:
            sent(3, yp * NZ + zz)
    for g in range(8):
        r_, c_ = b1_dest(g)

        @pl.when(jnp.logical_or(r_ != row, c_ != col))
        def _():
            b1_copy(g).wait_send()

    for d in range(1, 4):
        b2_copy(d).wait_send()


def local(pair, token_mask, w_query, w_key, w_value, w_gate, w_bias, *others):
    inputs = (pair, token_mask.reshape(1, -1), w_query, w_key, w_value, w_gate, w_bias.T, *others)
    rows_block, columns, channels = pair.shape
    hq = HEADS * columns
    cols = NY * NZ
    dma = pltpu.SemaphoreType.DMA
    return pl.pallas_call(
        functools.partial(kernel, columns),
        out_shape=jax.ShapeDtypeStruct((QR, columns, channels), BF16),
        in_specs=[pl.BlockSpec(memory_space=pltpu.HBM)] * 11,
        out_specs=pl.BlockSpec(memory_space=pltpu.VMEM),
        scratch_shapes=[pltpu.VMEM(array.shape, array.dtype) for array in inputs]
        + [
            pltpu.VMEM((cols, QR, columns, channels), BF16),
            pltpu.VMEM((8, 2, columns, channels), BF16),
            pltpu.VMEM((4, 8, columns, channels), BF16),
            pltpu.VMEM((CHUNKS, hq, cols * columns // CHUNKS), F32),
            pltpu.VMEM((QR, hq, channels), F32),
            pltpu.VMEM((QR, hq, channels), F32),
            pltpu.VMEM((QR, hq, channels), F32),
            pltpu.VMEM((QR, hq, channels), F32),
            pltpu.VMEM((2, columns, channels), BF16),
            dma((4, cols)),
            dma((cols,)),
            dma((8,)),
            dma((8,)),
            dma((4,)),
            dma((4,)),
            dma((12,)),
        ],
        compiler_params=pltpu.CompilerParams(
            collective_id=0, has_side_effects=True, vmem_limit_bytes=64 * 1024 * 1024
        ),
    )(*inputs)


def solution(mesh):
    return jax.shard_map(
        local,
        mesh=mesh,
        in_specs=(P("row", "col", None), P("col"), P(), P(), P(), P(), P(), P(), P(), P(), P()),
        out_specs=P("row", "col", None),
        check_vma=False,
    )
```

```python
import functools
import math

import jax
import jax.numpy as jnp
from jax import lax
from jax.experimental import pallas as pl
from jax.experimental.pallas import tpu as pltpu
from jax.sharding import PartitionSpec as P

HEADS = 4
HEAD_DIM = 32
QR = 20
NX = 4
NY = 4
NZ = 8
LINE = 2 * NZ
GROUP = QR // NY
JOINT = 1
DEAD = -1e30
MESH = pl.DeviceIdType.MESH
F32 = jnp.float32
BF16 = jnp.bfloat16


def normalize(values_in):
    average = jnp.mean(values_in, axis=-1, keepdims=True)
    centred = values_in - average
    variance = jnp.mean(centred * centred, axis=-1, keepdims=True)
    return centred * lax.rsqrt(variance + 1e-05)


def dot(a, b):
    return jnp.dot(a, b, preferred_element_type=F32)


def dot_t(a, b):
    return lax.dot_general(a, b, (((1,), (1,)), ((), ())), preferred_element_type=F32)


def sigmoid(v):
    return 1.0 / (1.0 + jnp.exp(-v))


def kernel(columns, *refs):
    inputs, out_ref, held = refs[:11], refs[11], refs[12:23]
    pair_ref, mask_ref, wq_ref, wk_ref, wv_ref, wg_ref, wb_ref, wo_ref, wha_ref, whb_ref, who_ref = held
    gath, own, gated_ref, back, turned, bias_all, bias_t, qk_ref, mean_ref = refs[23:32]
    send_o, send_g, recv_g, recv_p, send_r, recv_r, turn_sem, send_z, recv_z = refs[32:41]
    send_b, recv_b, core_sem, walk_sem, load_sem = refs[41:]
    rows_block, _, channels = pair_ref.shape
    tokens = QR * columns
    hq = HEADS * columns
    keys = NY * NZ * columns
    row = lax.axis_index("row")
    col = lax.axis_index("col")
    x, zh, core = row // 4, (row // 2) % 2, row % 2
    y, z = col // NZ, col % NZ
    place = zh * NZ + z

    def at_x(other):
        return other * 4 + zh * 2 + core, col

    def at_y(other):
        return row, other * NZ + z

    def at_place(other):
        return x * 4 + (other // NZ) * 2 + core, y * NZ + other % NZ

    sibling = (row + 1 - 2 * core, col)
    mirror = (y * 4 + zh * 2 + core, x * NZ + z)

    def load(n):
        if n == 0:
            return pltpu.make_async_copy(inputs[0].at[:QR], pair_ref.at[:QR], load_sem.at[0])
        if n == 11:
            rest_rows = pl.ds(QR, rows_block - QR)
            return pltpu.make_async_copy(inputs[0].at[rest_rows], pair_ref.at[rest_rows], load_sem.at[11])
        return pltpu.make_async_copy(inputs[n], held[n], load_sem.at[n])

    barrier = pltpu.get_barrier_semaphore()

    def tell(sem, target):
        pl.semaphore_signal(sem, inc=1, device_id=target, device_id_type=MESH)

    def either_side(distance, fn):
        @pl.when(place >= distance)
        def _():
            fn(0, place - distance)

        @pl.when(place + distance < LINE)
        def _():
            fn(1, place + distance)

    for d in range(1, NY):
        tell(barrier, at_y((y + d) % NY))
    for d in range(1, NX):
        tell(barrier, at_x((x + d) % NX))
    tell(barrier, sibling)

    @pl.when(x != y)
    def _():
        tell(barrier, mirror)

    either_side(1, lambda side, other: tell(barrier, at_place(other)))
    for n in (0, 11, 6, 1, 2, 3, 4, 5, 7, 8, 9, 10):
        load(n).start()
    load(0).wait()
    win = normalize(pair_ref[:QR].astype(F32)).astype(BF16)
    own[...] = win.reshape(NY, GROUP, columns, channels)
    gath[y, z] = own[y]
    greeted = (place > 0).astype(jnp.int32) + (place < LINE - 1).astype(jnp.int32) + (x != y).astype(jnp.int32)
    pl.semaphore_wait(barrier, NX + NY - 1 + greeted)

    def walk_tell(n):
        either_side(2**n, lambda side, other: tell(walk_sem.at[n, 1 - side], at_place(other)))

    def walk_wait(n):
        either_side(2**n, lambda side, other: pl.semaphore_wait(walk_sem.at[n, side], 1))

    def local_wait(ref, sem):
        pltpu.make_async_copy(ref, ref, sem).wait()

    def remote(src, dst, send, recv, target):
        return pltpu.make_async_remote_copy(
            src_ref=src, dst_ref=dst, send_sem=send, recv_sem=recv, device_id=target, device_id_type=MESH
        )

    def spread(other):
        return remote(own.at[other], gath.at[y, z], send_o.at[other], recv_g.at[y], at_y(other))

    def piece(p, zz):
        return gath.at[pl.ds(p * JOINT, JOINT), zz]

    def hop(side, p, zz):
        target = (row, col - 1 + 2 * side)
        return remote(piece(p, zz), piece(p, zz), send_g.at[side, p, zz], recv_p.at[p, zz], target)

    def begin(p):
        @pl.when(z < NZ - 1)
        def _():
            hop(1, p, z).start()

        @pl.when(z > 0)
        def _():
            hop(0, p, z).start()

    def step(t):
        def one(o, carry):
            p = (y // JOINT + o) % (NY // JOINT)

            @pl.when(z >= t)
            def _():
                local_wait(piece(p, z - t), recv_p.at[p, z - t])

                @pl.when(z < NZ - 1)
                def _():
                    hop(1, p, z - t).start()

            @pl.when(z + t < NZ)
            def _():
                local_wait(piece(p, z + t), recv_p.at[p, z + t])

                @pl.when(z > 0)
                def _():
                    hop(0, p, z + t).start()

            return carry

        lax.fori_loop(0, NY // JOINT, one, 0)

    walk_tell(0)
    begin(y)
    for d in (1, 3, 2):
        spread((y + d) % NY).start()

    lane = lax.broadcasted_iota(jnp.int32, (columns, channels), 1)
    head_of = sum((lane >= columns * (h + 1)).astype(jnp.int32) for h in range(HEADS))
    lane_mod = lane - head_of * columns
    for n in (11, 6, 1):
        load(n).wait()
    wb = wb_ref[...].astype(F32)
    wide = [jnp.broadcast_to(wb[h : h + 1], (columns, channels)) for h in range(HEADS)]
    wide = jnp.concatenate(wide + [jnp.zeros((channels - hq, channels), F32)], axis=0).astype(BF16)
    mask_row = mask_ref[...].astype(F32)
    eye = lax.broadcasted_iota(jnp.int32, (columns, columns), 0) == lax.broadcasted_iota(
        jnp.int32, (columns, columns), 1
    )
    alive = jnp.sum(jnp.where(eye, mask_row, 0.0), axis=1, keepdims=True)
    for half in range(2):
        normed = normalize(pair_ref[half * columns : (half + 1) * columns].astype(F32))
        full = dot_t(normed.reshape(columns * columns, channels).astype(BF16), wide)
        full = full.reshape(columns, columns, channels)
        picked = jnp.zeros((columns, channels), F32)
        for j in range(columns):
            picked = jnp.where(lane_mod == j, full[j], picked)
        picked = jnp.where(alive > 0.0, picked, DEAD)
        turned[0, half] = picked.astype(BF16)

    def turn():
        return remote(turned.at[0], turned.at[1], turn_sem.at[0], turn_sem.at[1], mirror)

    def z_place(half, far):
        return far * NZ + zh * 4 + core * 2 + half

    def copy_z(half, far):
        target = at_place(z_place(half, far))
        return remote(turned.at[1, half], bias_all.at[y, x, z], send_z.at[half, far], recv_z.at[z], target)

    low, high = pl.ds(0, NZ // 2), pl.ds(NZ // 2, NZ // 2)

    def plane(n, other):
        part = (
            bias_all.at[y, x, low],
            bias_all.at[y, x, high],
            bias_all.at[y, :, low],
            bias_all.at[:, x, high],
        )[n]
        mine = y if n in (1, 2) else x
        target = at_y(other) if n in (1, 2) else at_x(other)
        return remote(part, part, send_b.at[n, other], recv_b.at[n, mine], target)

    def plane_wait(n, other):
        part = (
            bias_all.at[y, other, low],
            bias_all.at[other, x, high],
            bias_all.at[other, :, low],
            bias_all.at[:, other, high],
        )[n]
        local_wait(part, recv_b.at[n, other])

    def others(n):
        return [((y if n in (1, 2) else x) + d) % NY for d in (1, 3, 2)]

    def copy_c():
        return remote(bias_all, bias_all, core_sem.at[0], core_sem.at[1], sibling)

    @pl.when(x != y)
    def _():
        turn().start()

    @pl.when(x == y)
    def _():
        pltpu.make_async_copy(turned.at[0], turned.at[1], turn_sem.at[1]).start()

    walk_wait(0)
    walk_tell(1)
    for d in (1, 3, 2):
        p = (y + d) % NY
        local_wait(gath.at[p, z], recv_g.at[p])
        begin(p)
    walk_wait(1)
    walk_tell(2)
    step(1)
    local_wait(turned.at[1], turn_sem.at[1])
    walk_wait(2)
    walk_tell(3)

    for n in (2, 3):
        load(n).wait()
    flat = gath[:, z].astype(F32).reshape(tokens, channels).astype(BF16)
    q = (dot(flat, wq_ref[...]) * (1.0 / math.sqrt(HEAD_DIM))).astype(BF16)
    lane_t = lax.broadcasted_iota(jnp.int32, (tokens, channels), 1)
    for h in range(HEADS):
        inside = jnp.logical_and(lane_t >= h * HEAD_DIM, lane_t < (h + 1) * HEAD_DIM)
        mine = jnp.where(inside, q.astype(F32), 0.0).astype(BF16)
        qk_h = dot_t(mine, wk_ref[...])
        qk_ref[:, :, h * columns : (h + 1) * columns, :] = qk_h.reshape(NY, GROUP, columns, channels)

    step(2)
    walk_wait(3)
    for half in range(2):
        for far in range(2):
            here = z_place(half, far) == place

            @pl.when(here)
            def _():
                pltpu.make_async_copy(turned.at[1, half], bias_all.at[y, x, z], recv_z.at[z]).start()

            @pl.when(jnp.logical_not(here))
            def _():
                copy_z(half, far).start()

    owner = core == (z // 2) % 2
    step(3)
    step(4)

    @pl.when(owner)
    def _():
        for zz in range(NZ):
            local_wait(bias_all.at[y, x, zz], recv_z.at[zz])
        for n in (0, 1):
            for other in others(n):
                plane(n, other).start()

    step(5)

    @pl.when(owner)
    def _():
        for n in (0, 1):
            for other in others(n):
                plane_wait(n, other)
        for n in (2, 3):
            for other in others(n):
                plane(n, other).start()

    step(6)

    @pl.when(owner)
    def _():
        for n in (2, 3):
            for other in others(n):
                plane_wait(n, other)
        copy_c().start()

    step(7)

    @pl.when(jnp.logical_not(owner))
    def _():
        local_wait(bias_all, core_sem.at[1])

    for n in range(NY):
        block = bias_all[n].astype(F32).reshape(keys, channels)
        bias_t[n] = jnp.swapaxes(block, 0, 1)[:hq]

    def attend(i, carry):
        block = gath[:, :, i].astype(F32).reshape(keys, channels).astype(BF16)
        for n in range(NY):
            s = dot_t(qk_ref[n, i].astype(BF16), block) + bias_t[n]
            prob = jnp.exp(s - jnp.max(s, axis=1, keepdims=True))
            total = jnp.sum(prob, axis=1, keepdims=True)
            mean_ref[n, i] = dot(prob.astype(BF16), block) / total
        return carry

    lax.fori_loop(0, GROUP, attend, 0)

    for n in (4, 5, 7, 8, 9, 10):
        load(n).wait()
    attended = jnp.zeros((tokens, channels), F32)
    for h in range(HEADS):
        mine = mean_ref[:, :, h * columns : (h + 1) * columns].reshape(tokens, channels).astype(BF16)
        inside = jnp.logical_and(lane_t >= h * HEAD_DIM, lane_t < (h + 1) * HEAD_DIM)
        attended = jnp.where(inside, dot(mine, wv_ref[...]), attended)
    flat = gath[:, z].astype(F32).reshape(tokens, channels).astype(BF16)
    gated = sigmoid(dot(flat, wg_ref[...])) * attended
    gated_ref[...] = gated.reshape(NY, GROUP, columns, channels).astype(BF16)

    def go_home(other):
        return remote(gated_ref.at[other], back.at[y], send_r.at[other], recv_r.at[y], at_y(other))

    for d in (1, 3, 2):
        go_home((y + d) % NY).start()
    back[y] = gated_ref[y]
    for d in (1, 3, 2):
        other = (y + d) % NY
        local_wait(back.at[other], recv_r.at[other])
    gated = back[...].astype(F32).reshape(tokens, channels).astype(BF16)
    first = pair_ref[:QR].astype(F32).reshape(tokens, channels) + dot(gated, wo_ref[...])
    normed_two = normalize(first).astype(BF16)
    a = dot(normed_two, wha_ref[...])
    b = dot(normed_two, whb_ref[...])
    hidden = (a * sigmoid(a) * b).astype(BF16)
    updated = first + dot(hidden, who_ref[...])
    out_ref[...] = updated.reshape(QR, columns, channels).astype(out_ref.dtype)

    for d in range(1, NY):
        spread((y + d) % NY).wait_send()
        go_home((y + d) % NY).wait_send()

    def left(p, carry):
        for zz in range(NZ):

            @pl.when(jnp.logical_and(zz <= z, z < NZ - 1))
            def _():
                local_wait(piece(p, zz), send_g.at[1, p, zz])

            @pl.when(jnp.logical_and(zz >= z, z > 0))
            def _():
                local_wait(piece(p, zz), send_g.at[0, p, zz])

        return carry

    lax.fori_loop(0, NY // JOINT, left, 0)

    @pl.when(x != y)
    def _():
        turn().wait_send()

    for half in range(2):
        for far in range(2):

            @pl.when(z_place(half, far) != place)
            def _():
                copy_z(half, far).wait_send()

    @pl.when(owner)
    def _():
        for n in range(4):
            for other in others(n):
                plane(n, other).wait_send()
        copy_c().wait_send()


def local(pair, token_mask, w_query, w_key, w_value, w_gate, w_bias, *others):
    inputs = (pair, token_mask.reshape(1, -1), w_query, w_key, w_value, w_gate, w_bias.T, *others)
    rows_block, columns, channels = pair.shape
    hq = HEADS * columns
    cols = NY * NZ
    dma = pltpu.SemaphoreType.DMA
    return pl.pallas_call(
        functools.partial(kernel, columns),
        out_shape=jax.ShapeDtypeStruct((QR, columns, channels), BF16),
        in_specs=[pl.BlockSpec(memory_space=pltpu.HBM)] * 11,
        out_specs=pl.BlockSpec(memory_space=pltpu.VMEM),
        scratch_shapes=[pltpu.VMEM(array.shape, array.dtype) for array in inputs]
        + [
            pltpu.VMEM((NY, NZ, GROUP, columns, channels), BF16),
            pltpu.VMEM((NY, GROUP, columns, channels), BF16),
            pltpu.VMEM((NY, GROUP, columns, channels), BF16),
            pltpu.VMEM((NY, GROUP, columns, channels), BF16),
            pltpu.VMEM((2, 2, columns, channels), BF16),
            pltpu.VMEM((NY, NX, NZ, columns, channels), BF16),
            pltpu.VMEM((NY, hq, cols * columns), F32),
            pltpu.VMEM((NY, GROUP, hq, channels), F32),
            pltpu.VMEM((NY, GROUP, hq, channels), F32),
            dma((NY,)),
            dma((2, NY // JOINT, NZ)),
            dma((NY,)),
            dma((NY // JOINT, NZ)),
            dma((NY,)),
            dma((NY,)),
            dma((2,)),
            dma((2, 2)),
            dma((NZ,)),
            dma((4, NY)),
            dma((4, NY)),
            dma((2,)),
            pltpu.SemaphoreType.REGULAR((4, 2)),
            dma((12,)),
        ],
        compiler_params=pltpu.CompilerParams(
            collective_id=0, has_side_effects=True, vmem_limit_bytes=48 * 1024 * 1024
        ),
    )(*[pltpu.with_memory_space_constraint(array, pltpu.HBM) for array in inputs])


def solution(mesh):
    return jax.shard_map(
        local,
        mesh=mesh,
        in_specs=(P("row", "col", None), P("col"), P(), P(), P(), P(), P(), P(), P(), P(), P()),
        out_specs=P("row", "col", None),
        check_vma=False,
    )
```

```python
import functools
import math

import jax
import jax.numpy as jnp
from jax import lax
from jax.experimental import pallas as pl
from jax.experimental.pallas import tpu as pltpu
from jax.sharding import PartitionSpec as P

HEADS = 4
HEAD_DIM = 32
QR = 20
NX = 4
NY = 4
NZ = 8
LINE = 2 * NZ
GROUP = QR // NY
JOINT = 1
DEAD = -1e30
MESH = pl.DeviceIdType.MESH
F32 = jnp.float32
BF16 = jnp.bfloat16


def normalize(values_in):
    average = jnp.mean(values_in, axis=-1, keepdims=True)
    centred = values_in - average
    variance = jnp.mean(centred * centred, axis=-1, keepdims=True)
    return centred * lax.rsqrt(variance + 1e-05)


def dot(a, b):
    return jnp.dot(a, b, preferred_element_type=F32)


def dot_t(a, b):
    return lax.dot_general(a, b, (((1,), (1,)), ((), ())), preferred_element_type=F32)


def sigmoid(v):
    return 1.0 / (1.0 + jnp.exp(-v))


def kernel(columns, *refs):
    inputs, out_ref, held = refs[:11], refs[11], refs[12:23]
    pair_ref, mask_ref, wq_ref, wk_ref, wv_ref, wg_ref, wb_ref, wo_ref, wha_ref, whb_ref, who_ref = held
    gath, own, gated_ref, back, turned, bias_all, bias_t, qk_ref, mean_ref = refs[23:32]
    send_o, send_g, recv_g, recv_p, send_r, recv_r, turn_sem, send_z, recv_z = refs[32:41]
    send_b, recv_b, send_c, recv_c, walk_sem, load_sem = refs[41:]
    rows_block, _, channels = pair_ref.shape
    tokens = QR * columns
    hq = HEADS * columns
    keys = NY * NZ * columns
    row = lax.axis_index("row")
    col = lax.axis_index("col")
    x, zh, core = row // 4, (row // 2) % 2, row % 2
    y, z = col // NZ, col % NZ
    place = zh * NZ + z

    def at_x(other):
        return other * 4 + zh * 2 + core, col

    def at_y(other):
        return row, other * NZ + z

    def at_place(other):
        return x * 4 + (other // NZ) * 2 + core, y * NZ + other % NZ

    sibling = (row + 1 - 2 * core, col)
    mirror = (y * 4 + zh * 2 + core, x * NZ + z)

    def load(n):
        if n == 0:
            return pltpu.make_async_copy(inputs[0].at[:QR], pair_ref.at[:QR], load_sem.at[0])
        if n == 11:
            rest_rows = pl.ds(QR, rows_block - QR)
            return pltpu.make_async_copy(inputs[0].at[rest_rows], pair_ref.at[rest_rows], load_sem.at[11])
        return pltpu.make_async_copy(inputs[n], held[n], load_sem.at[n])

    barrier = pltpu.get_barrier_semaphore()

    def tell(sem, target):
        pl.semaphore_signal(sem, inc=1, device_id=target, device_id_type=MESH)

    def either_side(distance, fn):
        @pl.when(place >= distance)
        def _():
            fn(0, place - distance)

        @pl.when(place + distance < LINE)
        def _():
            fn(1, place + distance)

    for d in range(1, NY):
        tell(barrier, at_y((y + d) % NY))
    for d in range(1, NX):
        tell(barrier, at_x((x + d) % NX))
    tell(barrier, sibling)

    @pl.when(x != y)
    def _():
        tell(barrier, mirror)

    either_side(1, lambda side, other: tell(barrier, at_place(other)))
    for n in (0, 11, 6, 1, 2, 3, 4, 5, 7, 8, 9, 10):
        load(n).start()
    load(0).wait()
    win = normalize(pair_ref[:QR].astype(F32)).astype(BF16)
    own[...] = win.reshape(NY, GROUP, columns, channels)
    gath[y, z] = own[y]
    greeted = (place > 0).astype(jnp.int32) + (place < LINE - 1).astype(jnp.int32) + (x != y).astype(jnp.int32)
    pl.semaphore_wait(barrier, NX + NY - 1 + greeted)

    def walk_tell(n):
        either_side(2**n, lambda side, other: tell(walk_sem.at[n, 1 - side], at_place(other)))

    def walk_wait(n):
        either_side(2**n, lambda side, other: pl.semaphore_wait(walk_sem.at[n, side], 1))

    def local_wait(ref, sem):
        pltpu.make_async_copy(ref, ref, sem).wait()

    def remote(src, dst, send, recv, target):
        return pltpu.make_async_remote_copy(
            src_ref=src, dst_ref=dst, send_sem=send, recv_sem=recv, device_id=target, device_id_type=MESH
        )

    def spread(other):
        return remote(own.at[other], gath.at[y, z], send_o.at[other], recv_g.at[y], at_y(other))

    def piece(p, zz):
        return gath.at[pl.ds(p * JOINT, JOINT), zz]

    def hop(side, p, zz):
        target = (row, col - 1 + 2 * side)
        return remote(piece(p, zz), piece(p, zz), send_g.at[side, p, zz], recv_p.at[p, zz], target)

    def begin(p):
        @pl.when(z < NZ - 1)
        def _():
            hop(1, p, z).start()

        @pl.when(z > 0)
        def _():
            hop(0, p, z).start()

    def step(t):
        def one(o, carry):
            p = (y // JOINT + o) % (NY // JOINT)

            @pl.when(z >= t)
            def _():
                local_wait(piece(p, z - t), recv_p.at[p, z - t])

                @pl.when(z < NZ - 1)
                def _():
                    hop(1, p, z - t).start()

            @pl.when(z + t < NZ)
            def _():
                local_wait(piece(p, z + t), recv_p.at[p, z + t])

                @pl.when(z > 0)
                def _():
                    hop(0, p, z + t).start()

            return carry

        lax.fori_loop(0, NY // JOINT, one, 0)

    walk_tell(0)
    begin(y)
    for d in (1, 3, 2):
        spread((y + d) % NY).start()

    lane = lax.broadcasted_iota(jnp.int32, (columns, channels), 1)
    head_of = sum((lane >= columns * (h + 1)).astype(jnp.int32) for h in range(HEADS))
    lane_mod = lane - head_of * columns
    for n in (11, 6, 1):
        load(n).wait()
    wb = wb_ref[...].astype(F32)
    wide = [jnp.broadcast_to(wb[h : h + 1], (columns, channels)) for h in range(HEADS)]
    wide = jnp.concatenate(wide + [jnp.zeros((channels - hq, channels), F32)], axis=0).astype(BF16)
    mask_row = mask_ref[...].astype(F32)
    eye = lax.broadcasted_iota(jnp.int32, (columns, columns), 0) == lax.broadcasted_iota(
        jnp.int32, (columns, columns), 1
    )
    alive = jnp.sum(jnp.where(eye, mask_row, 0.0), axis=1, keepdims=True)
    for half in range(2):
        normed = normalize(pair_ref[half * columns : (half + 1) * columns].astype(F32))
        full = dot_t(normed.reshape(columns * columns, channels).astype(BF16), wide)
        full = full.reshape(columns, columns, channels)
        picked = jnp.zeros((columns, channels), F32)
        for j in range(columns):
            picked = jnp.where(lane_mod == j, full[j], picked)
        picked = jnp.where(alive > 0.0, picked, DEAD)
        turned[0, half] = picked.astype(BF16)

    def turn():
        return remote(turned.at[0], turned.at[1], turn_sem.at[0], turn_sem.at[1], mirror)

    def z_place(half, far):
        return far * NZ + zh * 4 + core * 2 + half

    def copy_z(half, far):
        target = at_place(z_place(half, far))
        return remote(turned.at[1, half], bias_all.at[y, x, z], send_z.at[half, far], recv_z.at[z], target)

    low, high = pl.ds(0, NZ // 2), pl.ds(NZ // 2, NZ // 2)

    def plane(n, other):
        part = (
            bias_all.at[y, x, low],
            bias_all.at[y, x, high],
            bias_all.at[y, :, low],
            bias_all.at[:, x, high],
        )[n]
        mine = y if n in (1, 2) else x
        target = at_y(other) if n in (1, 2) else at_x(other)
        return remote(part, part, send_b.at[n, other], recv_b.at[n, mine], target)

    def plane_wait(n, other):
        part = (
            bias_all.at[y, other, low],
            bias_all.at[other, x, high],
            bias_all.at[other, :, low],
            bias_all.at[:, other, high],
        )[n]
        local_wait(part, recv_b.at[n, other])

    def others(n):
        return [((y if n in (1, 2) else x) + d) % NY for d in (1, 3, 2)]

    def across(n, other):
        return bias_all.at[:, other, high] if n else bias_all.at[other, :, low]

    def copy_c(n, other):
        return remote(across(n, other), across(n, other), send_c.at[n, other], recv_c.at[n, other], sibling)

    def line_send(half, far):
        here = z_place(half, far) == place

        @pl.when(here)
        def _():
            pltpu.make_async_copy(turned.at[1, half], bias_all.at[y, x, z], recv_z.at[z]).start()

        @pl.when(jnp.logical_not(here))
        def _():
            copy_z(half, far).start()

    @pl.when(x != y)
    def _():
        turn().start()

    @pl.when(x == y)
    def _():
        pltpu.make_async_copy(turned.at[0], turned.at[1], turn_sem.at[1]).start()

    walk_wait(0)
    walk_tell(1)
    for d in (1, 3, 2):
        p = (y + d) % NY
        local_wait(gath.at[p, z], recv_g.at[p])
        begin(p)
    walk_wait(1)
    walk_tell(2)
    local_wait(turned.at[1], turn_sem.at[1])
    walk_wait(2)
    walk_tell(3)
    for half in range(2):
        line_send(half, zh)
    step(1)

    for n in (2, 3):
        load(n).wait()
    flat = gath[:, z].astype(F32).reshape(tokens, channels).astype(BF16)
    q = (dot(flat, wq_ref[...]) * (1.0 / math.sqrt(HEAD_DIM))).astype(BF16)
    lane_t = lax.broadcasted_iota(jnp.int32, (tokens, channels), 1)
    for h in range(HEADS):
        inside = jnp.logical_and(lane_t >= h * HEAD_DIM, lane_t < (h + 1) * HEAD_DIM)
        mine = jnp.where(inside, q.astype(F32), 0.0).astype(BF16)
        qk_h = dot_t(mine, wk_ref[...])
        qk_ref[:, :, h * columns : (h + 1) * columns, :] = qk_h.reshape(NY, GROUP, columns, channels)

    step(2)
    walk_wait(3)
    for half in range(2):
        line_send(half, 1 - zh)
    owner = core == (z // 2) % 2
    soon = z // 4 == zh

    def plane_one():
        for zz in range(NZ):
            local_wait(bias_all.at[y, x, zz], recv_z.at[zz])
        for n in (0, 1):
            for other in others(n):
                plane(n, other).start()

    def plane_two():
        for n in (0, 1):
            for other in others(n):
                plane_wait(n, other)
        for n in (2, 3):
            for other in others(n):
                plane(n, other).start()
        copy_c(0, y).start()
        copy_c(1, x).start()

    def to_core():
        for d in range(NY - 1):
            for n in (2, 3):
                other = others(n)[d]
                plane_wait(n, other)
                copy_c(n - 2, other).start()

    def stage(t, fn):
        @pl.when(jnp.logical_and(owner, soon if t else jnp.logical_not(soon)))
        def _():
            fn()

    step(3)
    stage(1, plane_one)
    step(4)
    stage(0, plane_one)
    stage(1, plane_two)
    step(5)
    stage(0, plane_two)
    stage(1, to_core)
    step(6)
    stage(0, to_core)
    step(7)

    @pl.when(jnp.logical_not(owner))
    def _():
        for n in range(2):
            for other in range(NY):
                local_wait(across(n, other), recv_c.at[n, other])

    for n in range(NY):
        block = bias_all[n].astype(F32).reshape(keys, channels)
        bias_t[n] = jnp.swapaxes(block, 0, 1)[:hq]

    def attend(i):
        block = gath[:, :, i].astype(F32).reshape(keys, channels).astype(BF16)
        qk = qk_ref[:, i].reshape(NY * hq, channels).astype(BF16)
        s = dot_t(qk, block) + bias_t[...].reshape(NY * hq, keys)
        prob = jnp.exp(s - jnp.max(s, axis=1, keepdims=True))
        total = jnp.sum(prob, axis=1, keepdims=True)
        mean = dot(prob.astype(BF16), block) / total
        mean_ref[:, i] = mean.reshape(NY, hq, channels)

    for i in range(GROUP):
        attend(i)

    for n in (4, 5, 7, 8, 9, 10):
        load(n).wait()
    attended = jnp.zeros((tokens, channels), F32)
    for h in range(HEADS):
        mine = mean_ref[:, :, h * columns : (h + 1) * columns].reshape(tokens, channels).astype(BF16)
        inside = jnp.logical_and(lane_t >= h * HEAD_DIM, lane_t < (h + 1) * HEAD_DIM)
        attended = jnp.where(inside, dot(mine, wv_ref[...]), attended)
    flat = gath[:, z].astype(F32).reshape(tokens, channels).astype(BF16)
    gated = sigmoid(dot(flat, wg_ref[...])) * attended
    gated_ref[...] = gated.reshape(NY, GROUP, columns, channels).astype(BF16)

    def go_home(other):
        return remote(gated_ref.at[other], back.at[y], send_r.at[other], recv_r.at[y], at_y(other))

    for d in (1, 3, 2):
        go_home((y + d) % NY).start()
    back[y] = gated_ref[y]
    for d in (1, 3, 2):
        other = (y + d) % NY
        local_wait(back.at[other], recv_r.at[other])
    gated = back[...].astype(F32).reshape(tokens, channels).astype(BF16)
    first = pair_ref[:QR].astype(F32).reshape(tokens, channels) + dot(gated, wo_ref[...])
    normed_two = normalize(first).astype(BF16)
    a = dot(normed_two, wha_ref[...])
    b = dot(normed_two, whb_ref[...])
    hidden = (a * sigmoid(a) * b).astype(BF16)
    updated = first + dot(hidden, who_ref[...])
    out_ref[...] = updated.reshape(QR, columns, channels).astype(out_ref.dtype)

    for d in range(1, NY):
        spread((y + d) % NY).wait_send()
        go_home((y + d) % NY).wait_send()

    def left(p, carry):
        for zz in range(NZ):

            @pl.when(jnp.logical_and(zz <= z, z < NZ - 1))
            def _():
                local_wait(piece(p, zz), send_g.at[1, p, zz])

            @pl.when(jnp.logical_and(zz >= z, z > 0))
            def _():
                local_wait(piece(p, zz), send_g.at[0, p, zz])

        return carry

    lax.fori_loop(0, NY // JOINT, left, 0)

    @pl.when(x != y)
    def _():
        turn().wait_send()

    for half in range(2):
        for far in range(2):

            @pl.when(z_place(half, far) != place)
            def _():
                copy_z(half, far).wait_send()

    @pl.when(owner)
    def _():
        for n in range(4):
            for other in others(n):
                plane(n, other).wait_send()
        for n in range(2):
            for other in range(NY):
                copy_c(n, other).wait_send()


def local(pair, token_mask, w_query, w_key, w_value, w_gate, w_bias, *others):
    inputs = (pair, token_mask.reshape(1, -1), w_query, w_key, w_value, w_gate, w_bias.T, *others)
    rows_block, columns, channels = pair.shape
    hq = HEADS * columns
    cols = NY * NZ
    dma = pltpu.SemaphoreType.DMA
    return pl.pallas_call(
        functools.partial(kernel, columns),
        out_shape=jax.ShapeDtypeStruct((QR, columns, channels), BF16),
        in_specs=[pl.BlockSpec(memory_space=pltpu.HBM)] * 11,
        out_specs=pl.BlockSpec(memory_space=pltpu.VMEM),
        scratch_shapes=[pltpu.VMEM(array.shape, array.dtype) for array in inputs]
        + [
            pltpu.VMEM((NY, NZ, GROUP, columns, channels), BF16),
            pltpu.VMEM((NY, GROUP, columns, channels), BF16),
            pltpu.VMEM((NY, GROUP, columns, channels), BF16),
            pltpu.VMEM((NY, GROUP, columns, channels), BF16),
            pltpu.VMEM((2, 2, columns, channels), BF16),
            pltpu.VMEM((NY, NX, NZ, columns, channels), BF16),
            pltpu.VMEM((NY, hq, cols * columns), F32),
            pltpu.VMEM((NY, GROUP, hq, channels), F32),
            pltpu.VMEM((NY, GROUP, hq, channels), F32),
            dma((NY,)),
            dma((2, NY // JOINT, NZ)),
            dma((NY,)),
            dma((NY // JOINT, NZ)),
            dma((NY,)),
            dma((NY,)),
            dma((2,)),
            dma((2, 2)),
            dma((NZ,)),
            dma((4, NY)),
            dma((4, NY)),
            dma((2, NY)),
            dma((2, NY)),
            pltpu.SemaphoreType.REGULAR((4, 2)),
            dma((12,)),
        ],
        compiler_params=pltpu.CompilerParams(
            collective_id=0, has_side_effects=True, vmem_limit_bytes=48 * 1024 * 1024
        ),
    )(*[pltpu.with_memory_space_constraint(array, pltpu.HBM) for array in inputs])


def solution(mesh):
    return jax.shard_map(
        local,
        mesh=mesh,
        in_specs=(P("row", "col", None), P("col"), P(), P(), P(), P(), P(), P(), P(), P(), P()),
        out_specs=P("row", "col", None),
        check_vma=False,
    )
```

```python
import functools
import math

import jax
import jax.numpy as jnp
from jax import lax
from jax.experimental import pallas as pl
from jax.experimental.pallas import tpu as pltpu
from jax.sharding import PartitionSpec as P

HEADS = 4
HEAD_DIM = 32
QR = 20
NX = 4
NY = 4
NZ = 8
GROUP = QR // NY
JOINT = 1
DEAD = -1e30
MESH = pl.DeviceIdType.MESH
F32 = jnp.float32
BF16 = jnp.bfloat16


def normalize(values_in):
    average = jnp.mean(values_in, axis=-1, keepdims=True)
    centred = values_in - average
    variance = jnp.mean(centred * centred, axis=-1, keepdims=True)
    return centred * lax.rsqrt(variance + 1e-05)


def dot(a, b):
    return jnp.dot(a, b, preferred_element_type=F32)


def dot_t(a, b):
    return lax.dot_general(a, b, (((1,), (1,)), ((), ())), preferred_element_type=F32)


def sigmoid(v):
    return 1.0 / (1.0 + jnp.exp(-v))


def kernel(columns, *refs):
    inputs, out_ref, held = refs[:11], refs[11], refs[12:23]
    pair_ref, mask_ref, wq_ref, wk_ref, wv_ref, wg_ref, wb_ref, wo_ref, wha_ref, whb_ref, who_ref = held
    gath, own, gated_ref, back, turned, bias_all, bias_t, qk_ref, mean_ref = refs[23:32]
    send_o, send_g, recv_g, recv_p, send_r, recv_r, turn_sem, send_z, recv_z = refs[32:41]
    send_b, recv_b, send_c, recv_c, far_sem, ready_sem, load_sem = refs[41:]
    rows_block, _, channels = pair_ref.shape
    tokens = QR * columns
    hq = HEADS * columns
    keys = NY * NZ * columns
    row = lax.axis_index("row")
    col = lax.axis_index("col")
    x, zh, core = row // 4, (row // 2) % 2, row % 2
    y, z = col // NZ, col % NZ
    place = zh * NZ + z

    def at_x(other):
        return other * 4 + zh * 2 + core, col

    def at_y(other):
        return row, other * NZ + z

    def at_place(other):
        return x * 4 + (other // NZ) * 2 + core, y * NZ + other % NZ

    sibling = (row + 1 - 2 * core, col)
    mirror = (y * 4 + zh * 2 + core, x * NZ + z)

    def load(n):
        if n == 0:
            return pltpu.make_async_copy(inputs[0].at[:QR], pair_ref.at[:QR], load_sem.at[0])
        if n == 11:
            rest_rows = pl.ds(QR, rows_block - QR)
            return pltpu.make_async_copy(inputs[0].at[rest_rows], pair_ref.at[rest_rows], load_sem.at[11])
        return pltpu.make_async_copy(inputs[n], held[n], load_sem.at[n])

    barrier = pltpu.get_barrier_semaphore()

    def tell(sem, target):
        pl.semaphore_signal(sem, inc=1, device_id=target, device_id_type=MESH)

    def z_place(half, far):
        return far * NZ + zh * 4 + core * 2 + half

    owner = core == (z // 2) % 2
    near = z // 4 == zh
    giver = jnp.logical_and(owner, jnp.logical_and(z < NZ // 2, zh == 0))
    getter = jnp.logical_and(owner, jnp.logical_and(z < NZ // 2, zh == 1))

    @pl.when(jnp.logical_and(owner, near))
    def _():
        for zz in range(NZ):

            @pl.when(zz != z)
            def _():
                tell(barrier, at_place(zh * NZ + zz))

    @pl.when(jnp.logical_and(owner, jnp.logical_and(z >= NZ // 2, zh == 0)))
    def _():
        for zz in range(NZ):
            tell(barrier, at_place(NZ + zz))

    for d in range(1, NY):
        tell(barrier, at_y((y + d) % NY))
    for d in range(1, NX):
        tell(barrier, at_x((x + d) % NX))
    tell(barrier, sibling)

    @pl.when(x != y)
    def _():
        tell(barrier, mirror)


    @pl.when(z > 0)
    def _():
        tell(barrier, (row, col - 1))

    @pl.when(z < NZ - 1)
    def _():
        tell(barrier, (row, col + 1))

    @pl.when(giver)
    def _():
        tell(barrier, at_place(NZ + z))

    for n in (0, 11, 6, 1, 2, 3, 4, 5, 7, 8, 9, 10):
        load(n).start()
    load(0).wait()
    win = normalize(pair_ref[:QR].astype(F32)).astype(BF16)
    own[...] = win.reshape(NY, GROUP, columns, channels)
    gath[y, z] = own[y]
    greeted = (z > 0).astype(jnp.int32) + (z < NZ - 1).astype(jnp.int32) + (x != y).astype(jnp.int32)
    greeted = greeted + getter.astype(jnp.int32)
    greeted = greeted + 2 + 2 * zh - jnp.logical_and(owner, near).astype(jnp.int32)
    pl.semaphore_wait(barrier, NX + NY - 1 + greeted)

    def local_wait(ref, sem):
        pltpu.make_async_copy(ref, ref, sem).wait()

    def remote(src, dst, send, recv, target):
        return pltpu.make_async_remote_copy(
            src_ref=src, dst_ref=dst, send_sem=send, recv_sem=recv, device_id=target, device_id_type=MESH
        )

    def spread(other):
        return remote(own.at[other], gath.at[y, z], send_o.at[other], recv_g.at[y], at_y(other))

    def piece(p, zz):
        return gath.at[pl.ds(p * JOINT, JOINT), zz]

    def hop(side, p, zz):
        target = (row, col - 1 + 2 * side)
        return remote(piece(p, zz), piece(p, zz), send_g.at[side, p, zz], recv_p.at[p, zz], target)

    def begin(p):
        @pl.when(z < NZ - 1)
        def _():
            hop(1, p, z).start()

        @pl.when(z > 0)
        def _():
            hop(0, p, z).start()

    def step(t):
        def one(o, carry):
            p = (y // JOINT + o) % (NY // JOINT)

            @pl.when(z >= t)
            def _():
                local_wait(piece(p, z - t), recv_p.at[p, z - t])

                @pl.when(z < NZ - 1)
                def _():
                    hop(1, p, z - t).start()

            @pl.when(z + t < NZ)
            def _():
                local_wait(piece(p, z + t), recv_p.at[p, z + t])

                @pl.when(z > 0)
                def _():
                    hop(0, p, z + t).start()

            return carry

        lax.fori_loop(0, NY // JOINT, one, 0)

    @pl.when(getter)
    def _():
        tell(ready_sem, at_place(z))

    for d in (1, 3, 2):
        spread((y + d) % NY).start()
    begin(y)

    lane = lax.broadcasted_iota(jnp.int32, (columns, channels), 1)
    head_of = sum((lane >= columns * (h + 1)).astype(jnp.int32) for h in range(HEADS))
    lane_mod = lane - head_of * columns
    for n in (11, 6, 1):
        load(n).wait()
    wb = wb_ref[...].astype(F32)
    wide = [jnp.broadcast_to(wb[h : h + 1], (columns, channels)) for h in range(HEADS)]
    wide = jnp.concatenate(wide + [jnp.zeros((channels - hq, channels), F32)], axis=0).astype(BF16)
    mask_row = mask_ref[...].astype(F32)
    eye = lax.broadcasted_iota(jnp.int32, (columns, columns), 0) == lax.broadcasted_iota(
        jnp.int32, (columns, columns), 1
    )
    alive = jnp.sum(jnp.where(eye, mask_row, 0.0), axis=1, keepdims=True)
    for half in range(2):
        normed = normalize(pair_ref[half * columns : (half + 1) * columns].astype(F32))
        full = dot_t(normed.reshape(columns * columns, channels).astype(BF16), wide)
        full = full.reshape(columns, columns, channels)
        picked = jnp.zeros((columns, channels), F32)
        for j in range(columns):
            picked = jnp.where(lane_mod == j, full[j], picked)
        picked = jnp.where(alive > 0.0, picked, DEAD)
        turned[0, half] = picked.astype(BF16)

    def turn():
        return remote(turned.at[0], turned.at[1], turn_sem.at[0], turn_sem.at[1], mirror)

    def copy_z(half, far):
        target = at_place(z_place(half, far))
        return remote(turned.at[1, half], bias_all.at[y, x, z], send_z.at[half, far], recv_z.at[z], target)

    low, high = pl.ds(0, NZ // 2), pl.ds(NZ // 2, NZ // 2)

    def plane(n, other):
        part = (
            bias_all.at[y, x, low],
            bias_all.at[y, x, high],
            bias_all.at[y, :, low],
            bias_all.at[:, x, high],
        )[n]
        mine = y if n in (1, 2) else x
        target = at_y(other) if n in (1, 2) else at_x(other)
        return remote(part, part, send_b.at[n, other], recv_b.at[n, mine], target)

    def plane_wait(n, other):
        part = (
            bias_all.at[y, other, low],
            bias_all.at[other, x, high],
            bias_all.at[other, :, low],
            bias_all.at[:, other, high],
        )[n]
        local_wait(part, recv_b.at[n, other])

    def others(n):
        return [((y if n in (1, 2) else x) + d) % NY for d in (1, 3, 2)]

    def across(n, other):
        return bias_all.at[:, other, high] if n else bias_all.at[other, :, low]

    def copy_c(n, other):
        return remote(across(n, other), across(n, other), send_c.at[n, other], recv_c.at[n, other], sibling)

    def line_send(half, far):
        here = z_place(half, far) == place

        @pl.when(here)
        def _():
            pltpu.make_async_copy(turned.at[1, half], bias_all.at[y, x, z], recv_z.at[z]).start()

        @pl.when(jnp.logical_not(here))
        def _():
            copy_z(half, far).start()

    @pl.when(x != y)
    def _():
        turn().start()

    @pl.when(x == y)
    def _():
        pltpu.make_async_copy(turned.at[0], turned.at[1], turn_sem.at[1]).start()

    for d in (1, 3, 2):
        p = (y + d) % NY
        local_wait(gath.at[p, z], recv_g.at[p])
        begin(p)
    local_wait(turned.at[1], turn_sem.at[1])
    for half in range(2):
        line_send(half, zh)

    @pl.when(zh == 1)
    def _():
        for half in range(2):
            line_send(half, 0)

    step(1)

    for n in (2, 3):
        load(n).wait()
    flat = gath[:, z].astype(F32).reshape(tokens, channels).astype(BF16)
    q = (dot(flat, wq_ref[...]) * (1.0 / math.sqrt(HEAD_DIM))).astype(BF16)
    lane_t = lax.broadcasted_iota(jnp.int32, (tokens, channels), 1)
    for h in range(HEADS):
        inside = jnp.logical_and(lane_t >= h * HEAD_DIM, lane_t < (h + 1) * HEAD_DIM)
        mine = jnp.where(inside, q.astype(F32), 0.0).astype(BF16)
        qk_h = dot_t(mine, wk_ref[...])
        qk_ref[:, :, h * columns : (h + 1) * columns, :] = qk_h.reshape(NY, GROUP, columns, channels)

    def copy_far():
        return remote(bias_all.at[y, x], bias_all.at[y, x], far_sem.at[0], far_sem.at[1], at_place(NZ + z))

    def plane_one():
        @pl.when(jnp.logical_not(getter))
        def _():
            for zz in range(NZ):
                local_wait(bias_all.at[y, x, zz], recv_z.at[zz])

        @pl.when(giver)
        def _():
            pl.semaphore_wait(ready_sem, 1)
            copy_far().start()

        @pl.when(getter)
        def _():
            local_wait(bias_all.at[y, x], far_sem.at[1])

        for n in (0, 1):
            for other in others(n):
                plane(n, other).start()

    def plane_two():
        for n in (0, 1):
            for other in others(n):
                plane_wait(n, other)
        for n in (2, 3):
            for other in others(n):
                plane(n, other).start()
        copy_c(0, y).start()
        copy_c(1, x).start()

    def to_core():
        for d in range(NY - 1):
            for n in (2, 3):
                other = others(n)[d]
                plane_wait(n, other)
                copy_c(n - 2, other).start()

    def stage(kind, fn):
        this = (near, jnp.logical_and(z >= NZ // 2, zh == 0), jnp.logical_and(z < NZ // 2, zh == 1))[kind]

        @pl.when(jnp.logical_and(owner, this))
        def _():
            fn()

    def take_bias():
        @pl.when(jnp.logical_not(owner))
        def _():
            for n in range(2):
                for other in range(NY):
                    local_wait(across(n, other), recv_c.at[n, other])

        for n in range(NY):
            block = bias_all[n].astype(F32).reshape(keys, channels)
            bias_t[n] = jnp.swapaxes(block, 0, 1)[:hq]

    step(2)
    stage(0, plane_one)
    stage(2, plane_one)
    step(3)
    stage(0, plane_two)
    stage(1, plane_one)
    stage(2, plane_two)
    step(4)
    stage(1, plane_two)
    step(5)
    stage(0, to_core)
    stage(2, to_core)
    step(6)
    stage(1, to_core)

    @pl.when(near)
    def _():
        take_bias()

    step(7)

    @pl.when(jnp.logical_not(near))
    def _():
        take_bias()

    def attend(i):
        block = gath[:, :, i].astype(F32).reshape(keys, channels).astype(BF16)
        qk = qk_ref[:, i].reshape(NY * hq, channels).astype(BF16)
        s = dot_t(qk, block) + bias_t[...].reshape(NY * hq, keys)
        prob = jnp.exp(s - jnp.max(s, axis=1, keepdims=True))
        total = jnp.sum(prob, axis=1, keepdims=True)
        mean = dot(prob.astype(BF16), block) / total
        mean_ref[:, i] = mean.reshape(NY, hq, channels)

    for i in range(GROUP):
        attend(i)

    for n in (4, 5, 7, 8, 9, 10):
        load(n).wait()
    attended = jnp.zeros((tokens, channels), F32)
    for h in range(HEADS):
        mine = mean_ref[:, :, h * columns : (h + 1) * columns].reshape(tokens, channels).astype(BF16)
        inside = jnp.logical_and(lane_t >= h * HEAD_DIM, lane_t < (h + 1) * HEAD_DIM)
        attended = jnp.where(inside, dot(mine, wv_ref[...]), attended)
    flat = gath[:, z].astype(F32).reshape(tokens, channels).astype(BF16)
    gated = sigmoid(dot(flat, wg_ref[...])) * attended
    gated_ref[...] = gated.reshape(NY, GROUP, columns, channels).astype(BF16)

    def go_home(other):
        return remote(gated_ref.at[other], back.at[y], send_r.at[other], recv_r.at[y], at_y(other))

    for d in (1, 3, 2):
        go_home((y + d) % NY).start()
    back[y] = gated_ref[y]
    for d in (1, 3, 2):
        other = (y + d) % NY
        local_wait(back.at[other], recv_r.at[other])
    gated = back[...].astype(F32).reshape(tokens, channels).astype(BF16)
    first = pair_ref[:QR].astype(F32).reshape(tokens, channels) + dot(gated, wo_ref[...])
    normed_two = normalize(first).astype(BF16)
    a = dot(normed_two, wha_ref[...])
    b = dot(normed_two, whb_ref[...])
    hidden = (a * sigmoid(a) * b).astype(BF16)
    updated = first + dot(hidden, who_ref[...])
    out_ref[...] = updated.reshape(QR, columns, channels).astype(out_ref.dtype)

    for d in range(1, NY):
        spread((y + d) % NY).wait_send()
        go_home((y + d) % NY).wait_send()

    def left(p, carry):
        for zz in range(NZ):

            @pl.when(jnp.logical_and(zz <= z, z < NZ - 1))
            def _():
                local_wait(piece(p, zz), send_g.at[1, p, zz])

            @pl.when(jnp.logical_and(zz >= z, z > 0))
            def _():
                local_wait(piece(p, zz), send_g.at[0, p, zz])

        return carry

    lax.fori_loop(0, NY // JOINT, left, 0)

    @pl.when(x != y)
    def _():
        turn().wait_send()

    for half in range(2):
        for far in range(2):

            @pl.when(jnp.logical_and(z_place(half, far) != place, far <= zh))
            def _():
                copy_z(half, far).wait_send()

    @pl.when(giver)
    def _():
        copy_far().wait_send()

    @pl.when(owner)
    def _():
        for n in range(4):
            for other in others(n):
                plane(n, other).wait_send()
        for n in range(2):
            for other in range(NY):
                copy_c(n, other).wait_send()


def local(pair, token_mask, w_query, w_key, w_value, w_gate, w_bias, *others):
    inputs = (pair, token_mask.reshape(1, -1), w_query, w_key, w_value, w_gate, w_bias.T, *others)
    rows_block, columns, channels = pair.shape
    hq = HEADS * columns
    cols = NY * NZ
    dma = pltpu.SemaphoreType.DMA
    return pl.pallas_call(
        functools.partial(kernel, columns),
        out_shape=jax.ShapeDtypeStruct((QR, columns, channels), BF16),
        in_specs=[pl.BlockSpec(memory_space=pltpu.HBM)] * 11,
        out_specs=pl.BlockSpec(memory_space=pltpu.VMEM),
        scratch_shapes=[pltpu.VMEM(array.shape, array.dtype) for array in inputs]
        + [
            pltpu.VMEM((NY, NZ, GROUP, columns, channels), BF16),
            pltpu.VMEM((NY, GROUP, columns, channels), BF16),
            pltpu.VMEM((NY, GROUP, columns, channels), BF16),
            pltpu.VMEM((NY, GROUP, columns, channels), BF16),
            pltpu.VMEM((2, 2, columns, channels), BF16),
            pltpu.VMEM((NY, NX, NZ, columns, channels), BF16),
            pltpu.VMEM((NY, hq, cols * columns), F32),
            pltpu.VMEM((NY, GROUP, hq, channels), F32),
            pltpu.VMEM((NY, GROUP, hq, channels), F32),
            dma((NY,)),
            dma((2, NY // JOINT, NZ)),
            dma((NY,)),
            dma((NY // JOINT, NZ)),
            dma((NY,)),
            dma((NY,)),
            dma((2,)),
            dma((2, 2)),
            dma((NZ,)),
            dma((4, NY)),
            dma((4, NY)),
            dma((2, NY)),
            dma((2, NY)),
            dma((2,)),
            pltpu.SemaphoreType.REGULAR,
            dma((12,)),
        ],
        compiler_params=pltpu.CompilerParams(
            collective_id=0, has_side_effects=True, vmem_limit_bytes=48 * 1024 * 1024
        ),
    )(*[pltpu.with_memory_space_constraint(array, pltpu.HBM) for array in inputs])


def solution(mesh):
    return jax.shard_map(
        local,
        mesh=mesh,
        in_specs=(P("row", "col", None), P("col"), P(), P(), P(), P(), P(), P(), P(), P(), P()),
        out_specs=P("row", "col", None),
        check_vma=False,
    )
```

```python
import functools
import math

import jax
import jax.numpy as jnp
from jax import lax
from jax.experimental import pallas as pl
from jax.experimental.pallas import tpu as pltpu
from jax.sharding import PartitionSpec as P

HEADS = 4
HEAD_DIM = 32
QR = 20
NX = 4
NY = 4
NZ = 8
GROUP = QR // NY
JOINT = 1
DEAD = -1e30
MESH = pl.DeviceIdType.MESH
F32 = jnp.float32
BF16 = jnp.bfloat16


def normalize(values_in):
    average = jnp.mean(values_in, axis=-1, keepdims=True)
    centred = values_in - average
    variance = jnp.mean(centred * centred, axis=-1, keepdims=True)
    return centred * lax.rsqrt(variance + 1e-05)


def dot(a, b):
    return jnp.dot(a, b, preferred_element_type=F32)


def dot_t(a, b):
    return lax.dot_general(a, b, (((1,), (1,)), ((), ())), preferred_element_type=F32)


def sigmoid(v):
    return 1.0 / (1.0 + jnp.exp(-v))


def kernel(columns, *refs):
    inputs, out_ref, held = refs[:11], refs[11], refs[12:23]
    pair_ref, mask_ref, wq_ref, wk_ref, wv_ref, wg_ref, wb_ref, wo_ref, wha_ref, whb_ref, who_ref = held
    gath, own, gated_ref, back, turned, bias_all, bias_t, qk_ref, mean_ref, gate_ref = refs[23:33]
    send_o, send_g, recv_g, recv_p, send_r, recv_r, turn_sem, send_z, recv_z = refs[33:42]
    send_b, recv_b, send_c, recv_c, far_sem, ready_sem, load_sem = refs[42:]
    rows_block, _, channels = pair_ref.shape
    tokens = QR * columns
    hq = HEADS * columns
    keys = NY * NZ * columns
    row = lax.axis_index("row")
    col = lax.axis_index("col")
    x, zh, core = row // 4, (row // 2) % 2, row % 2
    y, z = col // NZ, col % NZ
    place = zh * NZ + z

    def at_x(other):
        return other * 4 + zh * 2 + core, col

    def at_y(other):
        return row, other * NZ + z

    def at_place(other):
        return x * 4 + (other // NZ) * 2 + core, y * NZ + other % NZ

    sibling = (row + 1 - 2 * core, col)
    mirror = (y * 4 + zh * 2 + core, x * NZ + z)

    def load(n):
        if n == 0:
            return pltpu.make_async_copy(inputs[0].at[:QR], pair_ref.at[:QR], load_sem.at[0])
        if n == 11:
            rest_rows = pl.ds(QR, rows_block - QR)
            return pltpu.make_async_copy(inputs[0].at[rest_rows], pair_ref.at[rest_rows], load_sem.at[11])
        return pltpu.make_async_copy(inputs[n], held[n], load_sem.at[n])

    barrier = pltpu.get_barrier_semaphore()

    def tell(sem, target):
        pl.semaphore_signal(sem, inc=1, device_id=target, device_id_type=MESH)

    def z_place(half, far):
        return far * NZ + zh * 4 + core * 2 + half

    owner = core == (z // 2) % 2
    near = z // 4 == zh
    giver = jnp.logical_and(owner, jnp.logical_and(z < NZ // 2, zh == 0))
    getter = jnp.logical_and(owner, jnp.logical_and(z < NZ // 2, zh == 1))

    @pl.when(jnp.logical_and(owner, near))
    def _():
        for zz in range(NZ):

            @pl.when(zz != z)
            def _():
                tell(barrier, at_place(zh * NZ + zz))

    @pl.when(jnp.logical_and(owner, jnp.logical_and(z >= NZ // 2, zh == 0)))
    def _():
        for zz in range(NZ):
            tell(barrier, at_place(NZ + zz))

    for d in range(1, NY):
        tell(barrier, at_y((y + d) % NY))
    for d in range(1, NX):
        tell(barrier, at_x((x + d) % NX))
    tell(barrier, sibling)

    @pl.when(x != y)
    def _():
        tell(barrier, mirror)


    @pl.when(z > 0)
    def _():
        tell(barrier, (row, col - 1))

    @pl.when(z < NZ - 1)
    def _():
        tell(barrier, (row, col + 1))

    @pl.when(giver)
    def _():
        tell(barrier, at_place(NZ + z))

    for n in (0, 11, 6, 1, 2, 3, 4, 5, 7, 8, 9, 10):
        load(n).start()
    load(0).wait()
    load(11).wait()
    normed_first = normalize(pair_ref[:columns].astype(F32))
    own[...] = normed_first[:QR].astype(BF16).reshape(NY, GROUP, columns, channels)
    gath[y, z] = own[y]
    lane = lax.broadcasted_iota(jnp.int32, (columns, channels), 1)
    head_of = sum((lane >= columns * (h + 1)).astype(jnp.int32) for h in range(HEADS))
    lane_mod = lane - head_of * columns
    for n in (6, 1):
        load(n).wait()
    wb = wb_ref[...].astype(F32)
    wide = [jnp.broadcast_to(wb[h : h + 1], (columns, channels)) for h in range(HEADS)]
    wide = jnp.concatenate(wide + [jnp.zeros((channels - hq, channels), F32)], axis=0).astype(BF16)
    mask_row = mask_ref[...].astype(F32)
    eye = lax.broadcasted_iota(jnp.int32, (columns, columns), 0) == lax.broadcasted_iota(
        jnp.int32, (columns, columns), 1
    )
    alive = jnp.sum(jnp.where(eye, mask_row, 0.0), axis=1, keepdims=True)
    for half in range(2):
        normed = normalize(pair_ref[columns:].astype(F32)) if half else normed_first
        full = dot_t(normed.reshape(columns * columns, channels).astype(BF16), wide)
        full = full.reshape(columns, columns, channels)
        picked = jnp.zeros((columns, channels), F32)
        for j in range(columns):
            picked = jnp.where(lane_mod == j, full[j], picked)
        picked = jnp.where(alive > 0.0, picked, DEAD)
        turned[0, half] = picked.astype(BF16)

    greeted = (z > 0).astype(jnp.int32) + (z < NZ - 1).astype(jnp.int32) + (x != y).astype(jnp.int32)
    greeted = greeted + getter.astype(jnp.int32)
    greeted = greeted + 2 + 2 * zh - jnp.logical_and(owner, near).astype(jnp.int32)
    pl.semaphore_wait(barrier, NX + NY - 1 + greeted)

    def local_wait(ref, sem):
        pltpu.make_async_copy(ref, ref, sem).wait()

    def remote(src, dst, send, recv, target):
        return pltpu.make_async_remote_copy(
            src_ref=src, dst_ref=dst, send_sem=send, recv_sem=recv, device_id=target, device_id_type=MESH
        )

    def spread(other):
        return remote(own.at[other], gath.at[y, z], send_o.at[other], recv_g.at[y], at_y(other))

    def piece(p, zz):
        return gath.at[pl.ds(p * JOINT, JOINT), zz]

    def hop(side, p, zz):
        target = (row, col - 1 + 2 * side)
        return remote(piece(p, zz), piece(p, zz), send_g.at[side, p, zz], recv_p.at[p, zz], target)

    def begin(p):
        @pl.when(z < NZ - 1)
        def _():
            hop(1, p, z).start()

        @pl.when(z > 0)
        def _():
            hop(0, p, z).start()

    def step(t):
        def one(o, carry):
            p = (y + jnp.where(o > 1, 5 - o, o)) % NY

            @pl.when(z >= t)
            def _():
                local_wait(piece(p, z - t), recv_p.at[p, z - t])

                @pl.when(z < NZ - 1)
                def _():
                    hop(1, p, z - t).start()

            @pl.when(z + t < NZ)
            def _():
                local_wait(piece(p, z + t), recv_p.at[p, z + t])

                @pl.when(z > 0)
                def _():
                    hop(0, p, z + t).start()

            return carry

        lax.fori_loop(0, NY // JOINT, one, 0)

    @pl.when(getter)
    def _():
        tell(ready_sem, at_place(z))

    for d in (1, 3, 2):
        spread((y + d) % NY).start()
    begin(y)

    def turn():
        return remote(turned.at[0], turned.at[1], turn_sem.at[0], turn_sem.at[1], mirror)

    def copy_z(half, far):
        target = at_place(z_place(half, far))
        return remote(turned.at[1, half], bias_all.at[y, x, z], send_z.at[half, far], recv_z.at[z], target)

    low, high = pl.ds(0, NZ // 2), pl.ds(NZ // 2, NZ // 2)

    def plane(n, other):
        part = (
            bias_all.at[y, x, low],
            bias_all.at[y, x, high],
            bias_all.at[y, :, low],
            bias_all.at[:, x, high],
        )[n]
        mine = y if n in (1, 2) else x
        target = at_y(other) if n in (1, 2) else at_x(other)
        return remote(part, part, send_b.at[n, other], recv_b.at[n, mine], target)

    def plane_wait(n, other):
        part = (
            bias_all.at[y, other, low],
            bias_all.at[other, x, high],
            bias_all.at[other, :, low],
            bias_all.at[:, other, high],
        )[n]
        local_wait(part, recv_b.at[n, other])

    def others(n):
        return [((y if n in (1, 2) else x) + d) % NY for d in (1, 3, 2)]

    def across(n, other):
        return bias_all.at[:, other, high] if n else bias_all.at[other, :, low]

    def copy_c(n, other):
        return remote(across(n, other), across(n, other), send_c.at[n, other], recv_c.at[n, other], sibling)

    def line_send(half, far):
        here = z_place(half, far) == place

        @pl.when(here)
        def _():
            pltpu.make_async_copy(turned.at[1, half], bias_all.at[y, x, z], recv_z.at[z]).start()

        @pl.when(jnp.logical_not(here))
        def _():
            copy_z(half, far).start()

    @pl.when(x != y)
    def _():
        turn().start()

    @pl.when(x == y)
    def _():
        pltpu.make_async_copy(turned.at[0], turned.at[1], turn_sem.at[1]).start()

    for d in (1, 3, 2):
        p = (y + d) % NY
        local_wait(gath.at[p, z], recv_g.at[p])
        begin(p)
    local_wait(turned.at[1], turn_sem.at[1])
    for half in range(2):
        line_send(half, zh)

    @pl.when(zh == 1)
    def _():
        for half in range(2):
            line_send(half, 0)

    step(1)

    for n in (2, 3, 5):
        load(n).wait()
    flat = gath[:, z].astype(F32).reshape(tokens, channels).astype(BF16)
    gate_ref[...] = sigmoid(dot(flat, wg_ref[...]))
    q = (dot(flat, wq_ref[...]) * (1.0 / math.sqrt(HEAD_DIM))).astype(BF16)
    lane_t = lax.broadcasted_iota(jnp.int32, (tokens, channels), 1)
    for h in range(HEADS):
        inside = jnp.logical_and(lane_t >= h * HEAD_DIM, lane_t < (h + 1) * HEAD_DIM)
        mine = jnp.where(inside, q.astype(F32), 0.0).astype(BF16)
        qk_h = dot_t(mine, wk_ref[...])
        qk_ref[:, :, h * columns : (h + 1) * columns, :] = qk_h.reshape(NY, GROUP, columns, channels)

    def copy_far():
        return remote(bias_all.at[y, x], bias_all.at[y, x], far_sem.at[0], far_sem.at[1], at_place(NZ + z))

    def plane_one():
        @pl.when(jnp.logical_not(getter))
        def _():
            for zz in range(NZ):
                local_wait(bias_all.at[y, x, zz], recv_z.at[zz])

        @pl.when(giver)
        def _():
            pl.semaphore_wait(ready_sem, 1)
            copy_far().start()

        @pl.when(getter)
        def _():
            local_wait(bias_all.at[y, x], far_sem.at[1])

        for n in (0, 1):
            for other in others(n):
                plane(n, other).start()

    def plane_two():
        for n in (0, 1):
            for other in others(n):
                plane_wait(n, other)
        for n in (2, 3):
            for other in others(n):
                plane(n, other).start()
        copy_c(0, y).start()
        copy_c(1, x).start()

    def to_core():
        for d in range(NY - 1):
            for n in (2, 3):
                other = others(n)[d]
                plane_wait(n, other)
                copy_c(n - 2, other).start()

    def stage(kind, fn):
        this = (near, jnp.logical_and(z >= NZ // 2, zh == 0), jnp.logical_and(z < NZ // 2, zh == 1))[kind]

        @pl.when(jnp.logical_and(owner, this))
        def _():
            fn()

    def take_bias():
        @pl.when(jnp.logical_not(owner))
        def _():
            for n in range(2):
                for other in range(NY):
                    local_wait(across(n, other), recv_c.at[n, other])

        for n in range(NY):
            block = bias_all[n].astype(F32).reshape(keys, channels)
            bias_t[n] = jnp.swapaxes(block, 0, 1)[:hq]

    step(2)
    stage(0, plane_one)
    stage(2, plane_one)
    step(3)
    stage(0, plane_two)
    stage(1, plane_one)
    stage(2, plane_two)
    step(4)
    stage(1, plane_two)
    step(5)
    stage(0, to_core)
    stage(2, to_core)
    step(6)
    stage(1, to_core)

    @pl.when(near)
    def _():
        take_bias()

    step(7)

    @pl.when(jnp.logical_not(near))
    def _():
        take_bias()

    def attend(i):
        block = gath[:, :, i].astype(F32).reshape(keys, channels).astype(BF16)
        qk = qk_ref[:, i].reshape(NY * hq, channels).astype(BF16)
        s = dot_t(qk, block) + bias_t[...].reshape(NY * hq, keys)
        prob = jnp.exp(s - jnp.max(s, axis=1, keepdims=True))
        total = jnp.sum(prob, axis=1, keepdims=True)
        mean = dot(prob.astype(BF16), block) / total
        mean_ref[:, i] = mean.reshape(NY, hq, channels)

    for i in range(GROUP):
        attend(i)

    for n in (4, 7, 8, 9, 10):
        load(n).wait()
    attended = jnp.zeros((tokens, channels), F32)
    for h in range(HEADS):
        mine = mean_ref[:, :, h * columns : (h + 1) * columns].reshape(tokens, channels).astype(BF16)
        inside = jnp.logical_and(lane_t >= h * HEAD_DIM, lane_t < (h + 1) * HEAD_DIM)
        attended = jnp.where(inside, dot(mine, wv_ref[...]), attended)
    gated = gate_ref[...] * attended
    gated_ref[...] = gated.reshape(NY, GROUP, columns, channels).astype(BF16)

    def go_home(other):
        return remote(gated_ref.at[other], back.at[y], send_r.at[other], recv_r.at[y], at_y(other))

    for d in (1, 3, 2):
        go_home((y + d) % NY).start()
    back[y] = gated_ref[y]
    for d in (1, 3, 2):
        other = (y + d) % NY
        local_wait(back.at[other], recv_r.at[other])
    gated = back[...].astype(F32).reshape(tokens, channels).astype(BF16)
    first = pair_ref[:QR].astype(F32).reshape(tokens, channels) + dot(gated, wo_ref[...])
    normed_two = normalize(first).astype(BF16)
    a = dot(normed_two, wha_ref[...])
    b = dot(normed_two, whb_ref[...])
    hidden = (a * sigmoid(a) * b).astype(BF16)
    updated = first + dot(hidden, who_ref[...])
    out_ref[...] = updated.reshape(QR, columns, channels).astype(out_ref.dtype)

    for d in range(1, NY):
        spread((y + d) % NY).wait_send()
        go_home((y + d) % NY).wait_send()

    def left(p, carry):
        for zz in range(NZ):

            @pl.when(jnp.logical_and(zz <= z, z < NZ - 1))
            def _():
                local_wait(piece(p, zz), send_g.at[1, p, zz])

            @pl.when(jnp.logical_and(zz >= z, z > 0))
            def _():
                local_wait(piece(p, zz), send_g.at[0, p, zz])

        return carry

    lax.fori_loop(0, NY // JOINT, left, 0)

    @pl.when(x != y)
    def _():
        turn().wait_send()

    for half in range(2):
        for far in range(2):

            @pl.when(jnp.logical_and(z_place(half, far) != place, far <= zh))
            def _():
                copy_z(half, far).wait_send()

    @pl.when(giver)
    def _():
        copy_far().wait_send()

    @pl.when(owner)
    def _():
        for n in range(4):
            for other in others(n):
                plane(n, other).wait_send()
        for n in range(2):
            for other in range(NY):
                copy_c(n, other).wait_send()


def local(pair, token_mask, w_query, w_key, w_value, w_gate, w_bias, *others):
    inputs = (pair, token_mask.reshape(1, -1), w_query, w_key, w_value, w_gate, w_bias.T, *others)
    rows_block, columns, channels = pair.shape
    hq = HEADS * columns
    cols = NY * NZ
    dma = pltpu.SemaphoreType.DMA
    return pl.pallas_call(
        functools.partial(kernel, columns),
        out_shape=jax.ShapeDtypeStruct((QR, columns, channels), BF16),
        in_specs=[pl.BlockSpec(memory_space=pltpu.HBM)] * 11,
        out_specs=pl.BlockSpec(memory_space=pltpu.VMEM),
        scratch_shapes=[pltpu.VMEM(array.shape, array.dtype) for array in inputs]
        + [
            pltpu.VMEM((NY, NZ, GROUP, columns, channels), BF16),
            pltpu.VMEM((NY, GROUP, columns, channels), BF16),
            pltpu.VMEM((NY, GROUP, columns, channels), BF16),
            pltpu.VMEM((NY, GROUP, columns, channels), BF16),
            pltpu.VMEM((2, 2, columns, channels), BF16),
            pltpu.VMEM((NY, NX, NZ, columns, channels), BF16),
            pltpu.VMEM((NY, hq, cols * columns), F32),
            pltpu.VMEM((NY, GROUP, hq, channels), F32),
            pltpu.VMEM((NY, GROUP, hq, channels), F32),
            pltpu.VMEM((QR * columns, channels), F32),
            dma((NY,)),
            dma((2, NY // JOINT, NZ)),
            dma((NY,)),
            dma((NY // JOINT, NZ)),
            dma((NY,)),
            dma((NY,)),
            dma((2,)),
            dma((2, 2)),
            dma((NZ,)),
            dma((4, NY)),
            dma((4, NY)),
            dma((2, NY)),
            dma((2, NY)),
            dma((2,)),
            pltpu.SemaphoreType.REGULAR,
            dma((12,)),
        ],
        compiler_params=pltpu.CompilerParams(
            collective_id=0, has_side_effects=True, vmem_limit_bytes=48 * 1024 * 1024
        ),
    )(*[pltpu.with_memory_space_constraint(array, pltpu.HBM) for array in inputs])


def solution(mesh):
    return jax.shard_map(
        local,
        mesh=mesh,
        in_specs=(P("row", "col", None), P("col"), P(), P(), P(), P(), P(), P(), P(), P(), P()),
        out_specs=P("row", "col", None),
        check_vma=False,
    )
```

```python
import functools
import math

import jax
import jax.numpy as jnp
from jax import lax
from jax.experimental import pallas as pl
from jax.experimental.pallas import tpu as pltpu
from jax.sharding import PartitionSpec as P

HEADS = 4
HEAD_DIM = 32
QR = 20
NX = 4
NY = 4
NZ = 8
GROUP = QR // NY
JOINT = 1
DEAD = -1e30
MESH = pl.DeviceIdType.MESH
F32 = jnp.float32
BF16 = jnp.bfloat16


def normalize(values_in):
    average = jnp.mean(values_in, axis=-1, keepdims=True)
    centred = values_in - average
    variance = jnp.mean(centred * centred, axis=-1, keepdims=True)
    return centred * lax.rsqrt(variance + 1e-05)


def dot(a, b):
    return jnp.dot(a, b, preferred_element_type=F32)


def dot_t(a, b):
    return lax.dot_general(a, b, (((1,), (1,)), ((), ())), preferred_element_type=F32)


def sigmoid(v):
    return 1.0 / (1.0 + jnp.exp(-v))


def kernel(columns, *refs):
    inputs, out_ref, held = refs[:11], refs[11], refs[12:23]
    pair_ref, mask_ref, wq_ref, wk_ref, wv_ref, wg_ref, wb_ref, wo_ref, wha_ref, whb_ref, who_ref = held
    gath, own, gated_ref, back, turned, bias_all, bias_t, qk_ref, mean_ref, gate_ref = refs[23:33]
    send_o, send_g, recv_g, recv_p, send_r, recv_r, turn_sem, send_z, recv_z = refs[33:42]
    send_b, recv_b, send_c, recv_c, far_sem, ready_sem, load_sem = refs[42:]
    rows_block, _, channels = pair_ref.shape
    tokens = QR * columns
    hq = HEADS * columns
    keys = NY * NZ * columns
    row = lax.axis_index("row")
    col = lax.axis_index("col")
    x, zh, core = row // 4, (row // 2) % 2, row % 2
    y, z = col // NZ, col % NZ
    place = zh * NZ + z

    def at_x(other):
        return other * 4 + zh * 2 + core, col

    def at_y(other):
        return row, other * NZ + z

    def at_place(other):
        return x * 4 + (other // NZ) * 2 + core, y * NZ + other % NZ

    sibling = (row + 1 - 2 * core, col)
    mirror = (y * 4 + zh * 2 + core, x * NZ + z)

    def load(n):
        if n == 0:
            return pltpu.make_async_copy(inputs[0].at[:QR], pair_ref.at[:QR], load_sem.at[0])
        if n == 11:
            rest_rows = pl.ds(QR, rows_block - QR)
            return pltpu.make_async_copy(inputs[0].at[rest_rows], pair_ref.at[rest_rows], load_sem.at[11])
        return pltpu.make_async_copy(inputs[n], held[n], load_sem.at[n])

    barrier = pltpu.get_barrier_semaphore()

    def tell(sem, target):
        pl.semaphore_signal(sem, inc=1, device_id=target, device_id_type=MESH)

    def z_place(half, far):
        return far * NZ + zh * 4 + core * 2 + half

    owner = core == (z // 2) % 2
    near = z // 4 == zh
    giver = jnp.logical_and(owner, jnp.logical_and(z < NZ // 2, zh == 0))
    getter = jnp.logical_and(owner, jnp.logical_and(z < NZ // 2, zh == 1))

    @pl.when(jnp.logical_and(owner, near))
    def _():
        for zz in range(NZ):

            @pl.when(zz != z)
            def _():
                tell(barrier, at_place(zh * NZ + zz))

    @pl.when(jnp.logical_and(owner, jnp.logical_and(z >= NZ // 2, zh == 0)))
    def _():
        for zz in range(NZ):
            tell(barrier, at_place(NZ + zz))

    for d in range(1, NY):
        tell(barrier, at_y((y + d) % NY))
    for d in range(1, NX):
        tell(barrier, at_x((x + d) % NX))
    tell(barrier, sibling)

    @pl.when(x != y)
    def _():
        tell(barrier, mirror)


    @pl.when(z > 0)
    def _():
        tell(barrier, (row, col - 1))

    @pl.when(z < NZ - 1)
    def _():
        tell(barrier, (row, col + 1))

    @pl.when(giver)
    def _():
        tell(barrier, at_place(NZ + z))

    for n in (0, 11, 6, 1, 2, 3, 4, 5, 7, 8, 9, 10):
        load(n).start()
    load(0).wait()
    load(11).wait()
    normed_first = normalize(pair_ref[:columns].astype(F32))
    own[...] = normed_first[:QR].astype(BF16).reshape(NY, GROUP, columns, channels)
    gath[y, z] = own[y]
    lane = lax.broadcasted_iota(jnp.int32, (columns, channels), 1)
    head_of = sum((lane >= columns * (h + 1)).astype(jnp.int32) for h in range(HEADS))
    lane_mod = lane - head_of * columns
    for n in (6, 1):
        load(n).wait()
    wb = wb_ref[...].astype(F32)
    wide = [jnp.broadcast_to(wb[h : h + 1], (columns, channels)) for h in range(HEADS)]
    wide = jnp.concatenate(wide + [jnp.zeros((channels - hq, channels), F32)], axis=0).astype(BF16)
    mask_row = mask_ref[...].astype(F32)
    eye = lax.broadcasted_iota(jnp.int32, (columns, columns), 0) == lax.broadcasted_iota(
        jnp.int32, (columns, columns), 1
    )
    alive = jnp.sum(jnp.where(eye, mask_row, 0.0), axis=1, keepdims=True)
    for half in range(2):
        normed = normalize(pair_ref[columns:].astype(F32)) if half else normed_first
        full = dot_t(normed.reshape(columns * columns, channels).astype(BF16), wide)
        full = full.reshape(columns, columns, channels)
        picked = jnp.zeros((columns, channels), F32)
        for j in range(columns):
            picked = jnp.where(lane_mod == j, full[j], picked)
        picked = jnp.where(alive > 0.0, picked, DEAD)
        turned[0, half] = picked.astype(BF16)

    greeted = (z > 0).astype(jnp.int32) + (z < NZ - 1).astype(jnp.int32) + (x != y).astype(jnp.int32)
    greeted = greeted + getter.astype(jnp.int32)
    greeted = greeted + 2 + 2 * zh - jnp.logical_and(owner, near).astype(jnp.int32)
    pl.semaphore_wait(barrier, NX + NY - 1 + greeted)

    def local_wait(ref, sem):
        pltpu.make_async_copy(ref, ref, sem).wait()

    def remote(src, dst, send, recv, target):
        return pltpu.make_async_remote_copy(
            src_ref=src, dst_ref=dst, send_sem=send, recv_sem=recv, device_id=target, device_id_type=MESH
        )

    def spread(other):
        return remote(own.at[other], gath.at[y, z], send_o.at[other], recv_g.at[y], at_y(other))

    def piece(p, zz):
        return gath.at[pl.ds(p * JOINT, JOINT), zz]

    def hop(side, p, zz):
        target = (row, col - 1 + 2 * side)
        return remote(piece(p, zz), piece(p, zz), send_g.at[side, p, zz], recv_p.at[p, zz], target)

    def begin(p):
        @pl.when(z < NZ - 1)
        def _():
            hop(1, p, z).start()

        @pl.when(z > 0)
        def _():
            hop(0, p, z).start()

    def step(t):
        def one(o, carry):
            p = (y + jnp.where(o > 1, 5 - o, o)) % NY

            @pl.when(z >= t)
            def _():
                local_wait(piece(p, z - t), recv_p.at[p, z - t])

                @pl.when(z < NZ - 1)
                def _():
                    hop(1, p, z - t).start()

            @pl.when(z + t < NZ)
            def _():
                local_wait(piece(p, z + t), recv_p.at[p, z + t])

                @pl.when(z > 0)
                def _():
                    hop(0, p, z + t).start()

            return carry

        lax.fori_loop(0, NY // JOINT, one, 0)

    @pl.when(getter)
    def _():
        tell(ready_sem, at_place(z))

    for d in (1, 3, 2):
        spread((y + d) % NY).start()
    begin(y)

    def turn():
        return remote(turned.at[0], turned.at[1], turn_sem.at[0], turn_sem.at[1], mirror)

    def copy_z(half, far):
        target = at_place(z_place(half, far))
        return remote(turned.at[1, half], bias_all.at[y, x, z], send_z.at[half, far], recv_z.at[z], target)

    low, high = pl.ds(0, NZ // 2), pl.ds(NZ // 2, NZ // 2)

    def plane(n, other):
        part = (
            bias_all.at[y, x, low],
            bias_all.at[y, x, high],
            bias_all.at[y, :, low],
            bias_all.at[:, x, high],
        )[n]
        mine = y if n in (1, 2) else x
        target = at_y(other) if n in (1, 2) else at_x(other)
        return remote(part, part, send_b.at[n, other], recv_b.at[n, mine], target)

    def plane_wait(n, other):
        part = (
            bias_all.at[y, other, low],
            bias_all.at[other, x, high],
            bias_all.at[other, :, low],
            bias_all.at[:, other, high],
        )[n]
        local_wait(part, recv_b.at[n, other])

    def others(n):
        return [((y if n in (1, 2) else x) + d) % NY for d in (1, 3, 2)]

    def across(n, other):
        return bias_all.at[:, other, high] if n else bias_all.at[other, :, low]

    def copy_c(n, other):
        return remote(across(n, other), across(n, other), send_c.at[n, other], recv_c.at[n, other], sibling)

    def line_send(half, far):
        here = z_place(half, far) == place

        @pl.when(here)
        def _():
            pltpu.make_async_copy(turned.at[1, half], bias_all.at[y, x, z], recv_z.at[z]).start()

        @pl.when(jnp.logical_not(here))
        def _():
            copy_z(half, far).start()

    @pl.when(x != y)
    def _():
        turn().start()

    @pl.when(x == y)
    def _():
        pltpu.make_async_copy(turned.at[0], turned.at[1], turn_sem.at[1]).start()

    for d in (1, 3, 2):
        p = (y + d) % NY
        local_wait(gath.at[p, z], recv_g.at[p])
        begin(p)
    local_wait(turned.at[1], turn_sem.at[1])
    for half in range(2):
        line_send(half, zh)

    @pl.when(zh == 1)
    def _():
        for half in range(2):
            line_send(half, 0)

    step(1)

    for n in (2, 3, 5):
        load(n).wait()
    flat = gath[:, z].astype(F32).reshape(tokens, channels).astype(BF16)
    gate_ref[...] = sigmoid(dot(flat, wg_ref[...]))
    q = (dot(flat, wq_ref[...]) * (1.0 / math.sqrt(HEAD_DIM))).astype(BF16)
    lane_t = lax.broadcasted_iota(jnp.int32, (tokens, channels), 1)
    for h in range(HEADS):
        inside = jnp.logical_and(lane_t >= h * HEAD_DIM, lane_t < (h + 1) * HEAD_DIM)
        mine = jnp.where(inside, q.astype(F32), 0.0).astype(BF16)
        qk_h = dot_t(mine, wk_ref[...])
        qk_ref[:, :, h * columns : (h + 1) * columns, :] = qk_h.reshape(NY, GROUP, columns, channels)

    def copy_far():
        return remote(bias_all.at[y, x], bias_all.at[y, x], far_sem.at[0], far_sem.at[1], at_place(NZ + z))

    def plane_one():
        @pl.when(jnp.logical_not(getter))
        def _():
            for zz in range(NZ):
                local_wait(bias_all.at[y, x, zz], recv_z.at[zz])

        @pl.when(giver)
        def _():
            pl.semaphore_wait(ready_sem, 1)
            copy_far().start()

        @pl.when(getter)
        def _():
            local_wait(bias_all.at[y, x], far_sem.at[1])

        for n in (0, 1):
            for other in others(n):
                plane(n, other).start()

    def plane_two():
        for n in (0, 1):
            for other in others(n):
                plane_wait(n, other)
        for n in (2, 3):
            for other in others(n):
                plane(n, other).start()
        copy_c(0, y).start()
        copy_c(1, x).start()

    def to_core():
        for d in range(NY - 1):
            for n in (2, 3):
                other = others(n)[d]
                plane_wait(n, other)
                copy_c(n - 2, other).start()

    def stage(kind, fn):
        this = (near, jnp.logical_and(z >= NZ // 2, zh == 0), jnp.logical_and(z < NZ // 2, zh == 1))[kind]

        @pl.when(jnp.logical_and(owner, this))
        def _():
            fn()

    def take_bias():
        @pl.when(jnp.logical_not(owner))
        def _():
            for n in range(2):
                for other in range(NY):
                    local_wait(across(n, other), recv_c.at[n, other])

        for n in range(NY):
            block = bias_all[n].astype(F32).reshape(keys, channels)
            bias_t[n] = jnp.swapaxes(block, 0, 1)[:hq]

    step(2)
    stage(0, plane_one)
    stage(2, plane_one)
    step(3)
    stage(0, plane_two)
    stage(1, plane_one)
    stage(2, plane_two)
    step(4)
    stage(1, plane_two)
    step(5)
    stage(0, to_core)
    stage(2, to_core)
    step(6)
    stage(1, to_core)

    @pl.when(near)
    def _():
        take_bias()

    step(7)

    @pl.when(jnp.logical_not(near))
    def _():
        take_bias()

    def attend(i):
        block = gath[:, :, i].astype(F32).reshape(keys, channels).astype(BF16)
        qk = qk_ref[:, i].reshape(NY * hq, channels).astype(BF16)
        s = dot_t(qk, block) + bias_t[...].reshape(NY * hq, keys)
        prob = jnp.exp(s - jnp.max(s, axis=1, keepdims=True))
        total = jnp.sum(prob, axis=1, keepdims=True)
        mean = dot(prob.astype(BF16), block) / total
        mean_ref[:, i] = mean.reshape(NY, hq, channels)

    for i in range(GROUP):
        attend(i)

    for n in (4, 7, 8, 9, 10):
        load(n).wait()
    count = GROUP * columns
    lane_c = lax.broadcasted_iota(jnp.int32, (count, channels), 1)

    def go_home(other):
        return remote(gated_ref.at[other], back.at[y], send_r.at[other], recv_r.at[y], at_y(other))

    for d in (2, 1, 3, 0):
        n = (y + d) % NY
        attended = jnp.zeros((count, channels), F32)
        for h in range(HEADS):
            mine = mean_ref[n, :, h * columns : (h + 1) * columns].reshape(count, channels).astype(BF16)
            inside = jnp.logical_and(lane_c >= h * HEAD_DIM, lane_c < (h + 1) * HEAD_DIM)
            attended = jnp.where(inside, dot(mine, wv_ref[...]), attended)
        gated = gate_ref[pl.ds(pl.multiple_of(n * count, 8), count)] * attended
        gated_ref[n] = gated.reshape(GROUP, columns, channels).astype(BF16)
        if d:
            go_home(n).start()
    back[y] = gated_ref[y]
    for d in (1, 3, 2):
        other = (y + d) % NY
        local_wait(back.at[other], recv_r.at[other])
    gated = back[...].astype(F32).reshape(tokens, channels).astype(BF16)
    first = pair_ref[:QR].astype(F32).reshape(tokens, channels) + dot(gated, wo_ref[...])
    normed_two = normalize(first).astype(BF16)
    a = dot(normed_two, wha_ref[...])
    b = dot(normed_two, whb_ref[...])
    hidden = (a * sigmoid(a) * b).astype(BF16)
    updated = first + dot(hidden, who_ref[...])
    out_ref[...] = updated.reshape(QR, columns, channels).astype(out_ref.dtype)

    for d in range(1, NY):
        spread((y + d) % NY).wait_send()
        go_home((y + d) % NY).wait_send()

    def left(p, carry):
        for zz in range(NZ):

            @pl.when(jnp.logical_and(zz <= z, z < NZ - 1))
            def _():
                local_wait(piece(p, zz), send_g.at[1, p, zz])

            @pl.when(jnp.logical_and(zz >= z, z > 0))
            def _():
                local_wait(piece(p, zz), send_g.at[0, p, zz])

        return carry

    lax.fori_loop(0, NY // JOINT, left, 0)

    @pl.when(x != y)
    def _():
        turn().wait_send()

    for half in range(2):
        for far in range(2):

            @pl.when(jnp.logical_and(z_place(half, far) != place, far <= zh))
            def _():
                copy_z(half, far).wait_send()

    @pl.when(giver)
    def _():
        copy_far().wait_send()

    @pl.when(owner)
    def _():
        for n in range(4):
            for other in others(n):
                plane(n, other).wait_send()
        for n in range(2):
            for other in range(NY):
                copy_c(n, other).wait_send()


def local(pair, token_mask, w_query, w_key, w_value, w_gate, w_bias, *others):
    inputs = (pair, token_mask.reshape(1, -1), w_query, w_key, w_value, w_gate, w_bias.T, *others)
    rows_block, columns, channels = pair.shape
    hq = HEADS * columns
    cols = NY * NZ
    dma = pltpu.SemaphoreType.DMA
    return pl.pallas_call(
        functools.partial(kernel, columns),
        out_shape=jax.ShapeDtypeStruct((QR, columns, channels), BF16),
        in_specs=[pl.BlockSpec(memory_space=pltpu.HBM)] * 11,
        out_specs=pl.BlockSpec(memory_space=pltpu.VMEM),
        scratch_shapes=[pltpu.VMEM(array.shape, array.dtype) for array in inputs]
        + [
            pltpu.VMEM((NY, NZ, GROUP, columns, channels), BF16),
            pltpu.VMEM((NY, GROUP, columns, channels), BF16),
            pltpu.VMEM((NY, GROUP, columns, channels), BF16),
            pltpu.VMEM((NY, GROUP, columns, channels), BF16),
            pltpu.VMEM((2, 2, columns, channels), BF16),
            pltpu.VMEM((NY, NX, NZ, columns, channels), BF16),
            pltpu.VMEM((NY, hq, cols * columns), F32),
            pltpu.VMEM((NY, GROUP, hq, channels), F32),
            pltpu.VMEM((NY, GROUP, hq, channels), F32),
            pltpu.VMEM((QR * columns, channels), F32),
            dma((NY,)),
            dma((2, NY // JOINT, NZ)),
            dma((NY,)),
            dma((NY // JOINT, NZ)),
            dma((NY,)),
            dma((NY,)),
            dma((2,)),
            dma((2, 2)),
            dma((NZ,)),
            dma((4, NY)),
            dma((4, NY)),
            dma((2, NY)),
            dma((2, NY)),
            dma((2,)),
            pltpu.SemaphoreType.REGULAR,
            dma((12,)),
        ],
        compiler_params=pltpu.CompilerParams(
            collective_id=0, has_side_effects=True, vmem_limit_bytes=48 * 1024 * 1024
        ),
    )(*[pltpu.with_memory_space_constraint(array, pltpu.HBM) for array in inputs])


def solution(mesh):
    return jax.shard_map(
        local,
        mesh=mesh,
        in_specs=(P("row", "col", None), P("col"), P(), P(), P(), P(), P(), P(), P(), P(), P()),
        out_specs=P("row", "col", None),
        check_vma=False,
    )
```
